128 devices in a mesh: gx: 16 (over x_lo, z, core), gy: 8 (over y, x_hi).
Axes of the slice: x: 4 (x_hi: 2, x_lo: 2; x = x_hi * 2 + x_lo), y: 4, z: 4, core: 2. Of those that a mesh axis runs over, the one named last changes fastest.
Arguments:
- electric: float32 [3, 16, 1024, 2048], P(None, None, 'gx', 'gy'), may hold values from -6 to 6
- magnetic: float32 [3, 16, 1024, 2048], P(None, None, 'gx', 'gy'), may hold values from -6 to 6
- inverse_permittivity: float32 [3, 16, 1024, 2048], P(None, None, 'gx', 'gy'), may hold values from 0.1 to 1
- forward_spectrum: float32 [4, 2, 3, 4, 1024, 2048], P(None, None, None, None, 'gx', 'gy'), may hold values from -6 to 6
- frequencies: float32 [4], replicated, may hold values from 0.3 to 1.2
- design_mask: int32 [4, 1024, 2048], P(None, 'gx', 'gy'), may hold values 0 or 1
- row_owner: int32 [1024, 1], replicated, may hold values from 0 to 15; in each aligned block of 64 rows (0 to 63, 64 to 127, ...) at most 8 rows name the same one
Outputs:
- electric_out: float32 [3, 16, 1024, 2048], P(None, None, 'gx', 'gy')
- magnetic_out: float32 [3, 16, 1024, 2048], P(None, None, 'gx', 'gy')
- owned_gradient: float32 [4, 4, 2048, 2048], P(None, None, 'gx', 'gy')
The draws below stay inside these ranges and needn't reach their ends.
Inputs may be any that keep to these rules, and one draw needn't show every extreme that they name: `row_owner`: in each aligned block of 64 rows (the rows of one tile along gx) no owner is named by more than 8 rows; in some block an owner is named by exactly 8 rows.
All inputs are finite; a program needn't handle non-finite values. No bound on the sum of `design_mask` on one device may be relied on, other than what follows from the above.
Results may differ from the reference program's by a relative error of at most 0.0003.
Values sent between devices are 32-bit elements; how exact they have to be, the bound alone decides.
A program may use at most 128 MiB of HBM per device.

```python
import math
import jax
import jax.numpy as jnp
import numpy as np
from jax import lax

NZ = 16
CX = 64
DP = 4
FREQ = 4
STEPS = 3
RADIUS = 3
NX = 1024
NY = 2048
SLOT_CAP = 8
N_GX = 16


def place_ends(entries, own_key, smallest, high):
    place = [jax.random.randint(jax.random.fold_in(own_key, axis), (), 0, length) for axis, length in enumerate(entries.shape)]
    main_axis = entries.shape.index(max(entries.shape))
    next_to = place[:main_axis] + [(place[main_axis] + 1) % entries.shape[main_axis]] + place[main_axis + 1:]
    return entries.at[tuple(place)].set(smallest).at[tuple(next_to)].set(high)


def level_of(own_key, dims, split, least, high):
    def one(dim, blocks):
        steps = jax.random.uniform(jax.random.fold_in(jax.random.fold_in(own_key, 6), dim), (blocks,), jnp.float32, least / len(split), high / len(split))
        return jnp.repeat(jnp.exp(steps), dims[dim] // blocks).reshape((-1,) + (1,) * (len(dims) - dim - 1))

    loudness = one(*split[0])
    for cut in split[1:]:
        loudness = loudness * one(*cut)
    return loudness


def routed_block(stream_key, own, number, rows, amount, top, reach, slope):
    order = jax.random.permutation(stream_key, amount)
    heavy_load, common = load_shares(amount, rows * top, reach, slope, True), load_shares(amount, rows * top, reach, slope, False)
    places = jnp.arange(amount)

    def named(sizes, offset_by):
        used = int((sizes > 0).sum())
        fixed = max(1, used // 4)
        moved = fixed + (places - fixed + offset_by * (used - fixed)) % max(1, amount - fixed)
        return jnp.zeros((amount,), jnp.int32).at[order[jnp.where(places < fixed, places, moved)]].set(jnp.asarray(sizes, jnp.int32))

    sizes = jnp.where(number % 4 == 0, named(heavy_load, number // 4), named(common, number - number // 4 - 1))
    mixed = jax.random.permutation(jax.random.fold_in(own, 3), amount)
    giver, receiver = mixed[0:amount // 2 * 2:2], mixed[1:amount // 2 * 2:2]
    margin = jnp.minimum(sizes[giver] - 1, reach - sizes[receiver]) // 2
    margin = jnp.where((giver == order[0]) | (receiver == order[0]) | (sizes[receiver] == 0), 0, jnp.maximum(margin, 0))
    moved = jax.random.randint(jax.random.fold_in(own, 4), (amount // 2,), 0, 1 << 20) % (margin + 1)
    sizes = sizes.at[giver].add(-moved).at[receiver].add(moved)
    labels = jnp.searchsorted(jnp.cumsum(sizes), jnp.arange(rows * top), side="right").astype(jnp.int32)
    table = labels.reshape(top, rows).T
    table = table[jax.random.permutation(jax.random.fold_in(own, 1), rows)]
    offset_by = jax.random.randint(jax.random.fold_in(own, 2), (rows, 1), 0, top)
    return jnp.take_along_axis(table, (jnp.arange(top)[None, :] + offset_by) % top, axis=1)


def load_shares(count, total, bound, lean, full):
    weights = [(1 << 20) // math.isqrt(rank ** lean) + 1 for rank in range(1, count + 1)]
    largest = bound if full else min(bound, max(-(-total // count), total * weights[0] // sum(weights)))
    least = 1 if total - largest >= count - 1 else 0
    counts, surplus = [largest] + [least] * (count - 1), total - largest - least * (count - 1)
    while surplus > 0:
        free = [i for i in range(1, count) if counts[i] < largest] or [i for i in range(1, count) if counts[i] < bound]
        pool, remaining = sum([weights[i] for i in free]), surplus
        for i in free:
            addition = min(bound - counts[i], max(1, remaining * weights[i] // pool), surplus)
            counts[i] = counts[i] + addition
            surplus = surplus - addition
    return np.array(counts)


def bell_draw(stream_key, dims, scale, reach, split=(), kind=jnp.bfloat16):
    entries = scale * jax.random.normal(stream_key, dims, jnp.float32)
    if split:
        entries = entries * level_of(stream_key, dims, split, -0.22, 0.18)
    return jnp.clip(entries, -reach, reach).astype(kind)


def setup_inputs(seed: int = 0) -> dict:
    key_list = jax.random.split(jax.random.key(seed), 8)
    electric = bell_draw(key_list[0], (3, NZ, NX, NY), 1.0, 6.0, ((2, 16), (3, 8)), jnp.float32)
    magnetic = bell_draw(key_list[1], (3, NZ, NX, NY), 1.0, 6.0, ((2, 16), (3, 8)), jnp.float32)
    inverse_permittivity = jnp.clip(jnp.exp(math.log(1.0) - 2.3025851 * jax.random.uniform(key_list[2], (3, NZ, NX, NY), jnp.float32) ** level_of(key_list[2], (3, NZ, NX, NY), ((2, 16), (3, 8)), -0.2, 0.2)), 0.1, 1.0)
    forward_spectrum = bell_draw(key_list[3], (FREQ, 2, 3, DP, NX, NY), 1.0, 6.0, ((4, 16), (5, 8)), jnp.float32)
    frequencies = jnp.clip(jax.random.uniform(key_list[4], (FREQ,), jnp.float32, 0.3, 1.2), 0.3, 1.2)
    design_mask = place_ends((jax.random.randint(key_list[5], (DP, NX, NY), 0, 4) < 3).astype(jnp.int32), jax.random.fold_in(key_list[5], 1), 0, 1)
    row_owner_keys = jax.random.split(jax.random.fold_in(key_list[6], 1), NX // CX)
    row_owner_turns = jax.random.permutation(jax.random.fold_in(key_list[6], 3), NX // CX)
    row_owner = jax.vmap(lambda own, number: routed_block(jax.random.fold_in(key_list[6], 2), own, number, CX, N_GX, 1, SLOT_CAP, 2))(row_owner_keys, row_owner_turns).reshape((NX, 1))
    return {"electric": electric, "magnetic": magnetic, "inverse_permittivity": inverse_permittivity, "forward_spectrum": forward_spectrum, "frequencies": frequencies, "design_mask": design_mask, "row_owner": row_owner}


COURANT = 0.5

def filter_table():
    table = []
    for shift_x in range(-RADIUS, RADIUS + 1):
        for shift_y in range(-RADIUS, RADIUS + 1):
            weight = RADIUS + 1.0 - math.sqrt(shift_x * shift_x + shift_y * shift_y)
            if weight > 0.0:
                table.append((shift_x, shift_y, weight))
    return table

def ahead(field, axis):
    padded = jnp.pad(field, [(0, 1) if index == axis else (0, 0) for index in range(3)])
    return lax.slice_in_dim(padded, 1, field.shape[axis] + 1, axis=axis) - field

def behind(field, axis):
    padded = jnp.pad(field, [(1, 0) if index == axis else (0, 0) for index in range(3)])
    return field - lax.slice_in_dim(padded, 0, field.shape[axis], axis=axis)

def advance(electric, magnetic, inverse):
    elec_x, elec_y, elec_z = (electric[0], electric[1], electric[2])
    magn_x = magnetic[0] - COURANT * (ahead(elec_z, 2) - ahead(elec_y, 0))
    magn_y = magnetic[1] - COURANT * (ahead(elec_x, 0) - ahead(elec_z, 1))
    magn_z = magnetic[2] - COURANT * (ahead(elec_y, 1) - ahead(elec_x, 2))
    elec_x = elec_x + COURANT * inverse[0] * (behind(magn_z, 2) - behind(magn_y, 0))
    elec_y = elec_y + COURANT * inverse[1] * (behind(magn_x, 0) - behind(magn_z, 1))
    elec_z = elec_z + COURANT * inverse[2] * (behind(magn_y, 1) - behind(magn_x, 2))
    return (jnp.stack([elec_x, elec_y, elec_z]), jnp.stack([magn_x, magn_y, magn_z]))

def reference(electric, magnetic, inverse_permittivity, forward_spectrum, frequencies, design_mask, row_owner):
    first = (NZ - DP) // 2
    raw = jnp.zeros((FREQ, DP, NX, NY), jnp.float32)
    for count in range(STEPS):
        electric, magnetic = advance(electric, magnetic, inverse_permittivity)
        design = electric[:, first:first + DP]
        phase = frequencies * (count + 1.0)
        cosine = jnp.cos(phase)
        sine = jnp.sin(phase)
        terms = []
        for freq in range(FREQ):
            weight = forward_spectrum[freq, 0] * cosine[freq] + forward_spectrum[freq, 1] * sine[freq]
            terms.append(lax.optimization_barrier(jnp.sum(weight * design, axis=0)))
        raw = raw + jnp.stack(terms)
    masked = raw * design_mask.astype(jnp.float32)[None]
    padded = jnp.pad(masked, ((0, 0), (0, 0), (RADIUS, RADIUS), (RADIUS, RADIUS)))
    ones = jnp.pad(jnp.ones((NX, NY), jnp.float32), RADIUS)
    total = jnp.zeros_like(masked)
    normal = jnp.zeros((NX, NY), jnp.float32)
    for shift_x, shift_y, weight in filter_table():
        total = total + weight * padded[:, :, RADIUS + shift_x:RADIUS + shift_x + NX, RADIUS + shift_y:RADIUS + shift_y + NY]
        normal = normal + weight * ones[RADIUS + shift_x:RADIUS + shift_x + NX, RADIUS + shift_y:RADIUS + shift_y + NY]
    filtered = total / normal
    owners = row_owner[:, 0].astype(jnp.int32)
    onehot = (owners[:, None] == jnp.arange(N_GX, dtype=jnp.int32)[None, :]).astype(jnp.int32)
    blocks = onehot.reshape(N_GX, CX, N_GX)
    before = jnp.cumsum(blocks, axis=1) - blocks
    position = lax.optimization_barrier(jnp.sum(before * blocks, axis=2)).reshape(NX).astype(jnp.int32)
    tiles = (jnp.arange(NX, dtype=jnp.int32) // CX).astype(jnp.int32)
    target = (owners * (N_GX * SLOT_CAP) + tiles * SLOT_CAP + position).astype(jnp.int32)
    owned = jnp.zeros((FREQ, DP, N_GX * N_GX * SLOT_CAP, NY), jnp.float32).at[:, :, target, :].set(filtered)
    return (electric, magnetic, owned)
```

```python
import functools
import math

import jax
import jax.numpy as jnp
from jax import lax
from jax.experimental import pallas as pl
from jax.experimental.pallas import tpu as pltpu
from jax.sharding import PartitionSpec as P

MESH = pl.DeviceIdType.MESH
F32 = jnp.float32

NZ = 16
ROWS = 64
COLS = 256
TOP = 8
LEFT = 128
XROWS = 80
XCOLS = 384
DP = 4
FIRST = 6
FREQ = 4
RADIUS = 3
CAP = 8
COURANT = 0.5

PIECES = (
    (0, 0, 3, 0), (0, 1, 3, 3), (2, 0, 2, 6),
    (0, 2, 3, 8), (1, 0, 3, 11), (2, 1, 2, 14),
    (1, 1, 3, 16), (1, 2, 3, 19), (2, 2, 2, 22),
)
INNER = tuple(range(3, 13))
OUTER = (0, 1, 2, 13, 14, 15)


def weight(shift_x, shift_y):
    return RADIUS + 1.0 - math.sqrt(shift_x * shift_x + shift_y * shift_y)


def roll(value, shift, axis):
    shift = shift % value.shape[axis]
    return value if shift == 0 else pltpu.roll(value, shift, axis)


def tile_rows(tile):
    return pl.ds(pl.multiple_of(tile * 8, 8), 8)


def kernel(
    n_x, n_y,
    elec_in, magn_in, perm_in, spec_in, freq_in, mask_in, owner_in,
    elec_out, magn_out, owned_out,
    elec, magn, perm, spec, mask, coef, trig, early, masked, inverse_norm, picker,
    fold, plane_out, packed,
    ysend_i, yrecv_i, xsend_i, xrecv_i,
    ysend_o, yrecv_o, xsend_o, xrecv_o,
    ysend_m, yrecv_m, xsend_m, xrecv_m,
    load_sem, save_sem, own_sem, send_sem, recv_sem, route_send, route_recv,
):
    gx = lax.axis_index("gx")
    gy = lax.axis_index("gy")
    x_up, x_down = lax.rem(gx + 1, n_x), lax.rem(gx + n_x - 1, n_x)
    y_up, y_down = lax.rem(gy + 1, n_y), lax.rem(gy + n_y - 1, n_y)

    own_r, own_c = pl.ds(TOP, ROWS), pl.ds(LEFT, COLS)

    def load(source, target, first, count, shift, sem):
        return pltpu.make_async_copy(
            source.at[:, pl.ds(first, count)],
            target.at[:, pl.ds(first + shift, count), own_r, own_c],
            load_sem.at[sem],
        )

    loads_i = [
        load(elec_in, elec, 3, 10, 0, 0),
        load(magn_in, magn, 3, 10, 1, 1),
        load(perm_in, perm, 3, 10, 0, 2),
    ]
    loads_o = [
        load(elec_in, elec, 0, 3, 0, 3), load(elec_in, elec, 13, 3, 0, 4),
        load(magn_in, magn, 0, 3, 1, 5), load(magn_in, magn, 13, 3, 1, 6),
        load(perm_in, perm, 0, 3, 0, 7), load(perm_in, perm, 13, 3, 0, 8),
    ]
    loads_s = [
        pltpu.make_async_copy(spec_in, spec, load_sem.at[9]),
        pltpu.make_async_copy(mask_in, mask, load_sem.at[10]),
    ]
    for copy in loads_i:
        copy.start()
    for copy in loads_o:
        copy.start()
    for copy in loads_s:
        copy.start()

    barrier = pltpu.get_barrier_semaphore()
    greeted = [(lax.rem(gx + k, n_x), gy) for k in range(1, n_x)]
    greeted += [(x, y) for x in (x_down, gx, x_up) for y in (y_down, y_up)]
    for peer in greeted:
        pl.semaphore_signal(barrier, inc=1, device_id=peer, device_id_type=MESH)

    lane = lax.broadcasted_iota(jnp.int32, (8, 128), 1)
    lanes = lax.broadcasted_iota(jnp.int32, (8, XCOLS), 1)
    sub3 = lax.broadcasted_iota(jnp.int32, (8, XCOLS), 0)
    sub = lax.broadcasted_iota(jnp.int32, (8, COLS), 0)
    has_down = jnp.where(gx > 0, 1.0, 0.0).astype(F32)
    has_up = jnp.where(gx < n_x - 1, 1.0, 0.0).astype(F32)
    has_left = jnp.where(gy > 0, 1.0, 0.0).astype(F32)
    has_right = jnp.where(gy < n_y - 1, 1.0, 0.0).astype(F32)

    for c in range(3):
        elec[c, NZ] = jnp.zeros((XROWS, XCOLS), F32)
        magn[c, 0] = jnp.zeros((XROWS, XCOLS), F32)

    half = jnp.where((lanes >= 64) & (lanes < 128), COURANT * has_left, COURANT)
    for t in range(10):
        coef[8 * t:8 * t + 8, :] = half * has_down if t == 0 else half

    for f in range(FREQ):
        for s in range(3):
            angle = jnp.full((8, 128), freq_in[f] * (s + 1.0), F32)
            trig[f, s, 0] = jnp.cos(angle)
            trig[f, s, 1] = jnp.sin(angle)

    col = gy * COLS + lax.broadcasted_iota(jnp.int32, (8, COLS), 1)
    inside = [
        ((col + b >= 0) & (col + b < n_y * COLS)).astype(F32) for b in range(-RADIUS, RADIUS + 1)
    ]
    sums = []
    for a in range(RADIUS + 1):
        total = jnp.zeros((8, COLS), F32)
        for b in range(-RADIUS, RADIUS + 1):
            if weight(a, b) > 0.0:
                total = total + weight(a, b) * inside[b + RADIUS]
        sums.append(total)

    def norm_tile(t, carry):
        row = gx * ROWS + t * 8 + sub
        total = jnp.zeros((8, COLS), F32)
        for a in range(-RADIUS, RADIUS + 1):
            within = ((row + a >= 0) & (row + a < n_x * ROWS)).astype(F32)
            total = total + within * sums[abs(a)]
        inverse_norm[tile_rows(t), :] = 1.0 / total
        return carry

    lax.fori_loop(0, ROWS // 8, norm_tile, 0)

    owners = owner_in[pl.ds(gx // 2, 1), :].astype(F32)
    lane1 = lax.broadcasted_iota(jnp.int32, (1, 128), 1)
    other = pltpu.roll(owners, 64, 1)
    low_half = lane1 < 64
    even = (lax.rem(gx, 2) == 0)
    keep = jnp.where(even, owners, other)
    swap = jnp.where(even, other, owners)
    owners = jnp.where(low_half, keep, pltpu.roll(keep, 64, 1))
    del swap
    rows_i = lax.broadcasted_iota(jnp.int32, (ROWS, 128), 0)
    lanes_j = lax.broadcasted_iota(jnp.int32, (ROWS, 128), 1)
    owners_b = jnp.broadcast_to(owners, (ROWS, 128))
    column = jnp.sum(jnp.where(rows_i == lanes_j, owners_b, 0.0), axis=1, keepdims=True)
    earlier = rows_i < jnp.where(lanes_j < 64, lanes_j, lanes_j - 64)
    same = jnp.where((column == owners_b) & earlier, 1.0, 0.0)
    slot = owners * CAP + jnp.sum(same, axis=0, keepdims=True)
    slots = jnp.concatenate([slot, slot], axis=1)
    wanted = lax.broadcasted_iota(jnp.int32, (n_x * CAP, 256), 0).astype(F32)
    used = lax.broadcasted_iota(jnp.int32, (n_x * CAP, 256), 1) < 3 * ROWS
    picker[...] = jnp.where((wanted == slots) & used, 1.0, 0.0).astype(jnp.bfloat16)

    fields = (elec, magn, perm)

    def plane_of(kind, p):
        return p + 1 if kind == 1 else p

    def pack(planes, at, ysend, xsend):
        def pack_y(t, carry):
            rows = pl.ds(pl.multiple_of(TOP + t * 8, 8), 8)
            for side in range(2):
                for group in range(2):
                    parts = jnp.zeros((8, 128), F32)
                    for i, p in enumerate(planes[5 * group:5 * group + 5]):
                        for kind, c, width, place in PIECES:
                            target = 24 * i + place
                            ref = fields[kind].at[c, plane_of(kind, p)]
                            if side == 0:
                                piece = ref[rows, pl.ds(2 * 128, 128)]
                                piece = roll(piece, target - (128 - width), 1)
                            else:
                                piece = ref[rows, pl.ds(128, 128)]
                                piece = roll(piece, target, 1)
                            parts = jnp.where(lane < target, parts, piece)
                    ysend[side, tile_rows(t), group * 128:group * 128 + 128] = parts
            return carry

        lax.fori_loop(0, ROWS // 8, pack_y, 0)

        def pack_x(q, carry):
            p = at(q)
            for side in range(2):
                start = TOP + ROWS - 8 if side == 0 else TOP
                for group in range(3):
                    parts = None
                    for kind, c, width, place in PIECES[3 * group:3 * group + 3]:
                        target = place - 8 * group
                        piece = fields[kind][c, plane_of(kind, p), start:start + 8, LEFT:XCOLS]
                        piece = roll(piece, target - (8 - width) if side == 0 else target, 0)
                        parts = piece if parts is None else jnp.where(sub < target, parts, piece)
                    xsend[side, q, 8 * group:8 * group + 8, :] = parts
            return carry

        lax.fori_loop(0, len(planes), pack_x, 0)

    def exchange(stage, ysend, yrecv, xsend, xrecv):
        plan = [
            (xsend.at[0], xrecv.at[0], (x_up, gy)),
            (xsend.at[1], xrecv.at[1], (x_down, gy)),
        ]
        for side, y in ((0, y_up), (1, y_down)):
            plan += [
                (ysend.at[side], yrecv.at[side, pl.ds(TOP, ROWS)], (gx, y)),
                (ysend.at[side, pl.ds(ROWS - 8, 8)], yrecv.at[side, pl.ds(0, 8)], (x_up, y)),
                (ysend.at[side, pl.ds(0, 8)], yrecv.at[side, pl.ds(TOP + ROWS, 8)], (x_down, y)),
            ]
        return [
            pltpu.make_async_remote_copy(
                src_ref=source, dst_ref=target,
                send_sem=send_sem.at[stage, i], recv_sem=recv_sem.at[stage, i],
                device_id=peer, device_id_type=MESH,
            )
            for i, (source, target, peer) in enumerate(plan)
        ]

    def unpack(planes, at, yrecv, xrecv):
        def unpack_y(t, carry):
            rows = tile_rows(t)
            there = jnp.where(t == 0, has_down, jnp.where(t == 9, has_up, 1.0))
            for group in range(2):
                if not planes[5 * group:5 * group + 5]:
                    continue
                cols = pl.ds(group * 128, 128)
                low = yrecv[0, rows, cols] * (there * has_left)
                high = yrecv[1, rows, cols] * (there * has_right)
                for i, p in enumerate(planes[5 * group:5 * group + 5]):
                    for kind, c, width, place in PIECES:
                        target = 24 * i + place
                        piece = jnp.where(
                            lane < 64, roll(high, -target, 1), roll(low, 128 - width - target, 1)
                        )
                        fields[kind].at[c, plane_of(kind, p)][rows, pl.ds(0, 128)] = piece
            return carry

        lax.fori_loop(0, XROWS // 8, unpack_y, 0)

        def unpack_x(q, carry):
            p = at(q)
            for side in range(2):
                start = 0 if side == 0 else TOP + ROWS
                for group in range(3):
                    parts = xrecv[side, q, 8 * group:8 * group + 8, :]
                    parts = parts * (has_down if side == 0 else has_up)
                    for kind, c, width, place in PIECES[3 * group:3 * group + 3]:
                        target = place - 8 * group
                        shift = 8 - width - target if side == 0 else -target
                        fields[kind][c, plane_of(kind, p), start:start + 8, LEFT:XCOLS] = roll(
                            parts, shift, 0
                        )
            return carry

        lax.fori_loop(0, len(planes), unpack_x, 0)

    def ahead_x(ref, c, p, t, value):
        if t == 9:
            return pltpu.roll(value, 7, 0)
        return pltpu.roll(jnp.where(sub3 == 0, ref[c, p, 8 * t + 8:8 * t + 16, :], value), 7, 0)

    def behind_x(ref, c, p, t, value):
        if t == 0:
            return pltpu.roll(value, 1, 0)
        return pltpu.roll(jnp.where(sub3 == 7, ref[c, p, 8 * t - 8:8 * t, :], value), 1, 0)

    def magnetic(start, stop):
        def one(p, carry):
            for t in range(10):
                rows = slice(8 * t, 8 * t + 8)
                ex, ey, ez = (elec[c, p, rows, :] for c in range(3))
                factor = coef[rows, :]
                ez_y = pltpu.roll(ez, XCOLS - 1, 1)
                ex_y = pltpu.roll(ex, XCOLS - 1, 1)
                ez_x = ahead_x(elec, 2, p, t, ez)
                ey_x = ahead_x(elec, 1, p, t, ey)
                q = p + 1
                magn[0, q, rows, :] -= factor * ((ez_y - ez) - (elec[1, q, rows, :] - ey))
                magn[1, q, rows, :] -= factor * ((elec[0, q, rows, :] - ex) - (ez_x - ez))
                magn[2, q, rows, :] -= factor * ((ey_x - ey) - (ex_y - ex))
            return carry

        lax.fori_loop(start, stop, one, 0)

    def electric(start, stop):
        def one(p, carry):
            for t in range(10):
                rows = slice(8 * t, 8 * t + 8)
                q = p + 1
                hx, hy, hz = (magn[c, q, rows, :] for c in range(3))
                hz_y = pltpu.roll(hz, 1, 1)
                hx_y = pltpu.roll(hx, 1, 1)
                hz_x = behind_x(magn, 2, q, t, hz)
                hy_x = behind_x(magn, 1, q, t, hy)
                elec[0, p, rows, :] += (COURANT * perm[0, p, rows, :]) * (
                    (hz - hz_y) - (hy - magn[1, p, rows, :])
                )
                elec[1, p, rows, :] += (COURANT * perm[1, p, rows, :]) * (
                    (hx - magn[0, p, rows, :]) - (hz - hz_x)
                )
                elec[2, p, rows, :] += (COURANT * perm[2, p, rows, :]) * (
                    (hy - hy_x) - (hx - hx_y)
                )
            return carry

        lax.fori_loop(start, stop, one, 0)

    for copy in loads_i:
        copy.wait()
    pack(INNER, lambda q: q + 3, ysend_i, xsend_i)
    pl.semaphore_wait(barrier, len(greeted))
    copies_i = exchange(0, ysend_i, yrecv_i, xsend_i, xrecv_i)
    for copy in copies_i:
        copy.start()
    for copy in loads_o:
        copy.wait()
    outer_at = lambda q: q + 10 * (q // 3)
    pack(OUTER, outer_at, ysend_o, xsend_o)
    for copy in copies_i:
        copy.wait()
    copies_o = exchange(1, ysend_o, yrecv_o, xsend_o, xrecv_o)
    for copy in copies_o:
        copy.start()
    unpack(INNER, lambda q: q + 3, yrecv_i, xrecv_i)

    for s in range(3):
        magnetic(3 + s, 12 - s)
        electric(4 + s, 12 - s)
        if s < 2:
            def keep_plane(p, carry, s=s):
                for c in range(3):
                    early[s, c, p] = elec[c, FIRST + p, TOP:TOP + ROWS, LEFT:XCOLS]
                return carry

            lax.fori_loop(0, DP, keep_plane, 0)

    for copy in loads_s:
        copy.wait()

    def gradient(k, carry):
        p, t = k // 8, lax.rem(k, 8)
        rows = tile_rows(t)
        ext = pl.ds(pl.multiple_of(TOP + t * 8, 8), 8)
        for h in range(2):
            cols = slice(128 * h, 128 * h + 128)
            far = slice(LEFT + 128 * h, LEFT + 128 * h + 128)
            fields_e = [
                [early[0, c, p, rows, cols], early[1, c, p, rows, cols], elec[c, FIRST + p, ext, far]]
                for c in range(3)
            ]
            keep = mask[p, rows, cols].astype(F32)
            for f in range(FREQ):
                total = jnp.zeros((8, 128), F32)
                for part in range(2):
                    w1, w2, w3 = (trig[f, s, part] for s in range(3))
                    for c in range(3):
                        e1, e2, e3 = fields_e[c]
                        total = total + spec[f, part, c, p, rows, cols] * (
                            w1 * e1 + w2 * e2 + w3 * e3
                        )
                masked[f * DP + p, ext, far] = total * keep
        return carry

    lax.fori_loop(0, DP * 8, gradient, 0)

    def edges_y(t, carry):
        ext = pl.ds(pl.multiple_of(TOP + t * 8, 8), 8)
        for side in range(2):
            parts = jnp.zeros((8, 128), F32)
            for m in range(FREQ * DP):
                if side == 0:
                    piece = roll(masked[m, ext, 256:384], 3 * m + 3, 1)
                else:
                    piece = roll(masked[m, ext, 128:256], 3 * m, 1)
                parts = jnp.where(lane < 3 * m, parts, piece)
            ysend_m[side, tile_rows(t), :] = parts
        return carry

    lax.fori_loop(0, ROWS // 8, edges_y, 0)

    def edges_x(j, carry):
        for side in range(2):
            start = TOP + ROWS - 8 if side == 0 else TOP
            first = masked[2 * j, start:start + 8, LEFT:XCOLS]
            second = pltpu.roll(masked[2 * j + 1, start:start + 8, LEFT:XCOLS], 3, 0)
            if side == 0:
                parts = jnp.where(sub < 3, second, first)
            else:
                parts = jnp.where(sub < 3, first, second)
            xsend_m[side, tile_rows(j), :] = parts
        return carry

    lax.fori_loop(0, FREQ * DP // 2, edges_x, 0)

    copies_m = exchange(2, ysend_m, yrecv_m, xsend_m, xrecv_m)
    for copy in copies_m:
        copy.start()
    for copy in copies_m:
        copy.wait()

    def put_y(t, carry):
        rows = tile_rows(t)
        there = jnp.where(t == 0, has_down, jnp.where(t == 9, has_up, 1.0))
        low = yrecv_m[0, rows, :] * (there * has_left)
        high = yrecv_m[1, rows, :] * (there * has_right)
        for m in range(FREQ * DP):
            masked[m, rows, 0:128] = jnp.where(
                lane < 64, roll(high, -3 * m, 1), roll(low, 125 - 3 * m, 1)
            )
        return carry

    lax.fori_loop(0, XROWS // 8, put_y, 0)

    def put_x(j, carry):
        for side in range(2):
            start = 0 if side == 0 else TOP + ROWS
            parts = xrecv_m[side, tile_rows(j), :] * (has_down if side == 0 else has_up)
            masked[2 * j, start:start + 8, LEFT:XCOLS] = parts
            masked[2 * j + 1, start:start + 8, LEFT:XCOLS] = pltpu.roll(parts, 5, 0)
        return carry

    lax.fori_loop(0, FREQ * DP // 2, put_x, 0)

    routes = []
    for f in range(FREQ):
        def filter_plane(p, carry, f=f):
            m = f * DP + p
            for t in range(10):
                value = masked[m, 8 * t:8 * t + 8, :]
                center = value[:, LEFT:XCOLS]
                pairs = [
                    (pltpu.roll(value, b, 1) + pltpu.roll(value, XCOLS - b, 1))[:, LEFT:XCOLS]
                    for b in range(1, RADIUS + 1)
                ]
                for a in range(RADIUS + 1):
                    if a == 0 and t in (0, 9):
                        continue
                    total = weight(a, 0) * center
                    for b in range(1, RADIUS + 1):
                        if weight(a, b) > 0.0:
                            total = total + weight(a, b) * pairs[b - 1]
                    fold[a, 8 * t:8 * t + 8, :] = total
            for t in range(1, 9):
                total = fold[0, 8 * t:8 * t + 8, :]
                for a in range(1, RADIUS + 1):
                    here = fold[a, 8 * t:8 * t + 8, :]
                    after = fold[a, 8 * t + 8:8 * t + 16, :]
                    before = fold[a, 8 * t - 8:8 * t, :]
                    total = total + pltpu.roll(jnp.where(sub < a, after, here), 8 - a, 0)
                    total = total + pltpu.roll(jnp.where(sub >= 8 - a, before, here), a, 0)
                plane_out[8 * t - 8:8 * t, :] = total * inverse_norm[8 * t - 8:8 * t, :]
            value = plane_out[...]
            high = value.astype(jnp.bfloat16)
            rest = value - high.astype(F32)
            middle = rest.astype(jnp.bfloat16)
            low = (rest - middle.astype(F32)).astype(jnp.bfloat16)
            stacked = jnp.concatenate([high, middle, low, jnp.zeros_like(low)], axis=0)
            packed[f, p] = jnp.dot(picker[...], stacked, preferred_element_type=F32)
            return carry

        lax.fori_loop(0, DP, filter_plane, 0)
        mine = pl.ds(pl.multiple_of(gx * CAP, CAP), CAP)
        for k in list(range(n_x // 2, n_x)) + list(range(1, n_x // 2)):
            owner = gx ^ k
            theirs = pl.ds(pl.multiple_of(owner * CAP, CAP), CAP)
            copy = pltpu.make_async_remote_copy(
                src_ref=packed.at[f, :, theirs], dst_ref=owned_out.at[f, :, mine],
                send_sem=route_send.at[f, k], recv_sem=route_recv.at[f, k],
                device_id=(owner, gy), device_id_type=MESH,
            )
            copy.start()
            routes.append(copy)
        copy = pltpu.make_async_copy(packed.at[f, :, mine], owned_out.at[f, :, mine], own_sem.at[f])
        copy.start()
        routes.append(copy)

    for copy in copies_o:
        copy.wait()
    unpack(OUTER, outer_at, yrecv_o, xrecv_o)
    for s in range(3):
        magnetic(12 - s, NZ)
        magnetic(0, 3 + s)
        electric(12 - s, NZ)
        electric(0, 4 + s)
    saves = [
        pltpu.make_async_copy(elec.at[:, pl.ds(0, NZ), own_r, own_c], elec_out, save_sem.at[0]),
        pltpu.make_async_copy(magn.at[:, pl.ds(1, NZ), own_r, own_c], magn_out, save_sem.at[1]),
    ]
    for copy in saves:
        copy.start()
    for copy in routes:
        copy.wait()
    for copy in saves:
        copy.wait()


def body(n_x, n_y, elec, magn, perm, spec, freq, mask, owner):
    any_space = pl.BlockSpec(memory_space=pl.ANY)
    vmem = pl.BlockSpec(memory_space=pltpu.VMEM)
    smem = pl.BlockSpec(memory_space=pltpu.SMEM)
    buf = pltpu.VMEM
    sem = pltpu.SemaphoreType.DMA
    return pl.pallas_call(
        functools.partial(kernel, n_x, n_y),
        out_shape=(
            jax.ShapeDtypeStruct((3, NZ, ROWS, COLS), F32),
            jax.ShapeDtypeStruct((3, NZ, ROWS, COLS), F32),
            jax.ShapeDtypeStruct((FREQ, DP, n_x * CAP, COLS), F32),
        ),
        in_specs=[any_space] * 4 + [smem, any_space, vmem],
        out_specs=(OUT_SPACE, OUT_SPACE, OUT_SPACE),
        scratch_shapes=[
            buf((3, NZ + 1, XROWS, XCOLS), F32),
            buf((3, NZ + 1, XROWS, XCOLS), F32),
            buf((3, NZ, XROWS, XCOLS), F32),
            buf((FREQ, 2, 3, DP, ROWS, COLS), F32),
            buf((DP, ROWS, COLS), jnp.int32),
            buf((XROWS, XCOLS), F32),
            buf((FREQ, 3, 2, 8, 128), F32),
            buf((2, 3, DP, ROWS, COLS), F32),
            buf((FREQ * DP, XROWS, XCOLS), F32),
            buf((ROWS, COLS), F32),
            buf((n_x * CAP, 256), jnp.bfloat16),
            buf((RADIUS + 1, XROWS, COLS), F32),
            buf((ROWS, COLS), F32),
            buf((FREQ, DP, n_x * CAP, COLS), F32),
            buf((2, ROWS, 256), F32), buf((2, XROWS, 256), F32),
            buf((2, len(INNER), 24, COLS), F32), buf((2, len(INNER), 24, COLS), F32),
            buf((2, ROWS, 256), F32), buf((2, XROWS, 256), F32),
            buf((2, len(OUTER), 24, COLS), F32), buf((2, len(OUTER), 24, COLS), F32),
            buf((2, ROWS, 128), F32), buf((2, XROWS, 128), F32),
            buf((2, ROWS, COLS), F32), buf((2, ROWS, COLS), F32),
            sem((11,)), sem((2,)), sem((FREQ,)), sem((3, 8)), sem((3, 8)),
            sem((FREQ, n_x)), sem((FREQ, n_x)),
        ],
        compiler_params=pltpu.CompilerParams(
            collective_id=0, has_side_effects=True, vmem_limit_bytes=52 << 20
        ),
        name="adjoint",
    )(elec, magn, perm, spec, freq, mask, owner.reshape(8, 128))


OUT_SPACE = pl.BlockSpec(memory_space=pl.ANY)


def solution(mesh):
    placed = (
        P(None, None, "gx", "gy"),
        P(None, None, "gx", "gy"),
        P(None, None, "gx", "gy"),
        P(None, None, None, None, "gx", "gy"),
        P(),
        P(None, "gx", "gy"),
        P(),
    )
    return jax.shard_map(
        functools.partial(body, mesh.shape["gx"], mesh.shape["gy"]),
        mesh=mesh,
        in_specs=placed,
        out_specs=(P(None, None, "gx", "gy"), P(None, None, "gx", "gy"), P(None, None, "gx", "gy")),
        check_vma=False,
    )
```

```python
import functools
import math

import jax
import jax.numpy as jnp
from jax import lax
from jax.experimental import pallas as pl
from jax.experimental.pallas import tpu as pltpu
from jax.sharding import PartitionSpec as P

MESH = pl.DeviceIdType.MESH
F32 = jnp.float32

NZ = 16
ROWS = 64
COLS = 256
TOP = 8
LEFT = 128
XROWS = 80
XCOLS = 384
DP = 4
FIRST = 6
FREQ = 4
RADIUS = 3
CAP = 8
COURANT = 0.5

PIECES = (
    (0, 0, 3, 0), (0, 1, 3, 3), (2, 0, 2, 6),
    (0, 2, 3, 8), (1, 0, 3, 11), (2, 1, 2, 14),
    (1, 1, 3, 16), (1, 2, 3, 19), (2, 2, 2, 22),
)
INNER = tuple(range(3, 13))
OUTER = (0, 1, 2, 13, 14, 15)


def weight(shift_x, shift_y):
    return RADIUS + 1.0 - math.sqrt(shift_x * shift_x + shift_y * shift_y)


def roll(value, shift, axis):
    shift = shift % value.shape[axis]
    return value if shift == 0 else pltpu.roll(value, shift, axis)


def tile_rows(tile):
    return pl.ds(pl.multiple_of(tile * 8, 8), 8)


def kernel(
    n_x, n_y,
    elec_in, magn_in, perm_in, spec_in, freq_hbm, mask_in, owner_hbm,
    elec, magn, owned_out,
    perm, spec, freq_in, mask, owner_in, trig, early, masked, inverse_norm, picker,
    fold, plane_out, packed,
    ysend_i, yrecv_i, xsend_i, xrecv_i,
    ysend_o, yrecv_o, xsend_o, xrecv_o,
    ysend_m, yrecv_m, xsend_m, xrecv_m,
    load_sem, own_sem, send_sem, recv_sem, route_send, route_recv,
):
    gx = lax.axis_index("gx")
    gy = lax.axis_index("gy")
    x_up, x_down = lax.rem(gx + 1, n_x), lax.rem(gx + n_x - 1, n_x)
    y_up, y_down = lax.rem(gy + 1, n_y), lax.rem(gy + n_y - 1, n_y)

    own_r, own_c = pl.ds(TOP, ROWS), pl.ds(LEFT, COLS)

    def load(source, target, first, count, shift, sem):
        return pltpu.make_async_copy(
            source.at[:, pl.ds(first, count)],
            target.at[:, pl.ds(first + shift, count), own_r, own_c],
            load_sem.at[sem],
        )

    loads_i = [
        load(elec_in, elec, 3, 10, 0, 0),
        load(magn_in, magn, 3, 10, 1, 1),
        load(perm_in, perm, 3, 10, 0, 2),
    ]
    loads_o = [
        load(elec_in, elec, 0, 3, 0, 3), load(elec_in, elec, 13, 3, 0, 4),
        load(magn_in, magn, 0, 3, 1, 5), load(magn_in, magn, 13, 3, 1, 6),
        load(perm_in, perm, 0, 3, 0, 7), load(perm_in, perm, 13, 3, 0, 8),
    ]
    loads_s = [
        pltpu.make_async_copy(spec_in, spec, load_sem.at[9]),
        pltpu.make_async_copy(mask_in, mask, load_sem.at[10]),
    ]
    loads_t = [
        pltpu.make_async_copy(freq_hbm, freq_in, load_sem.at[11]),
        pltpu.make_async_copy(owner_hbm, owner_in, load_sem.at[12]),
    ]
    for copy in loads_t:
        copy.start()
    for copy in loads_i:
        copy.start()
    for copy in loads_o:
        copy.start()
    for copy in loads_s:
        copy.start()

    barrier = pltpu.get_barrier_semaphore()
    greeted = [(lax.rem(gx + k, n_x), gy) for k in range(1, n_x)]
    greeted += [(x, y) for x in (x_down, gx, x_up) for y in (y_down, y_up)]
    for peer in greeted:
        pl.semaphore_signal(barrier, inc=1, device_id=peer, device_id_type=MESH)

    lane = lax.broadcasted_iota(jnp.int32, (8, 128), 1)
    lanes = lax.broadcasted_iota(jnp.int32, (8, XCOLS), 1)
    sub3 = lax.broadcasted_iota(jnp.int32, (8, XCOLS), 0)
    sub = lax.broadcasted_iota(jnp.int32, (8, COLS), 0)
    has_down = jnp.where(gx > 0, 1.0, 0.0).astype(F32)
    has_up = jnp.where(gx < n_x - 1, 1.0, 0.0).astype(F32)
    has_left = jnp.where(gy > 0, 1.0, 0.0).astype(F32)
    has_right = jnp.where(gy < n_y - 1, 1.0, 0.0).astype(F32)

    fields = (elec, magn, perm)

    half = jnp.where((lanes >= 64) & (lanes < 128), COURANT * has_left, COURANT)
    corner = half * has_down

    def plane_of(kind, p):
        return p + 1 if kind == 1 else p

    def pack_rows_y(planes, ysend):
        def pack_y(t, carry):
            rows = pl.ds(pl.multiple_of(TOP + t * 8, 8), 8)
            for side in range(2):
                for group in range(2):
                    parts = jnp.zeros((8, 128), F32)
                    for i, p in enumerate(planes[5 * group:5 * group + 5]):
                        for kind, c, width, place in PIECES:
                            target = 24 * i + place
                            ref = fields[kind].at[c, plane_of(kind, p)]
                            if side == 0:
                                piece = ref[rows, pl.ds(2 * 128, 128)]
                                piece = roll(piece, target - (128 - width), 1)
                            else:
                                piece = ref[rows, pl.ds(128, 128)]
                                piece = roll(piece, target, 1)
                            parts = jnp.where(lane < target, parts, piece)
                    ysend[side, tile_rows(t), group * 128:group * 128 + 128] = parts
            return carry

        lax.fori_loop(0, ROWS // 8, pack_y, 0)

    def pack_rows_x(planes, at, xsend):
        def pack_x(q, carry):
            p = at(q)
            for side in range(2):
                start = TOP + ROWS - 8 if side == 0 else TOP
                for group in range(3):
                    parts = None
                    for kind, c, width, place in PIECES[3 * group:3 * group + 3]:
                        target = place - 8 * group
                        piece = fields[kind][c, plane_of(kind, p), start:start + 8, LEFT:XCOLS]
                        piece = roll(piece, target - (8 - width) if side == 0 else target, 0)
                        parts = piece if parts is None else jnp.where(sub < target, parts, piece)
                    xsend[side, q, 8 * group:8 * group + 8, :] = parts
            return carry

        lax.fori_loop(0, len(planes), pack_x, 0)

    def exchange(stage, ysend, yrecv, xsend, xrecv):
        plan = [
            (xsend.at[0], xrecv.at[0], (x_up, gy)),
            (xsend.at[1], xrecv.at[1], (x_down, gy)),
        ]
        for side, y in ((0, y_up), (1, y_down)):
            plan += [
                (ysend.at[side], yrecv.at[side, pl.ds(TOP, ROWS)], (gx, y)),
                (ysend.at[side, pl.ds(ROWS - 8, 8)], yrecv.at[side, pl.ds(0, 8)], (x_up, y)),
                (ysend.at[side, pl.ds(0, 8)], yrecv.at[side, pl.ds(TOP + ROWS, 8)], (x_down, y)),
            ]
        return [
            pltpu.make_async_remote_copy(
                src_ref=source, dst_ref=target,
                send_sem=send_sem.at[stage, i], recv_sem=recv_sem.at[stage, i],
                device_id=peer, device_id_type=MESH,
            )
            for i, (source, target, peer) in enumerate(plan)
        ]

    def unpack_rows_y(planes, yrecv):
        def unpack_y(t, carry):
            rows = tile_rows(t)
            there = jnp.where(t == 0, has_down, jnp.where(t == 9, has_up, 1.0))
            for group in range(2):
                if not planes[5 * group:5 * group + 5]:
                    continue
                cols = pl.ds(group * 128, 128)
                low = yrecv[0, rows, cols] * (there * has_left)
                high = yrecv[1, rows, cols] * (there * has_right)
                for i, p in enumerate(planes[5 * group:5 * group + 5]):
                    for kind, c, width, place in PIECES:
                        target = 24 * i + place
                        piece = jnp.where(
                            lane < 64, roll(high, -target, 1), roll(low, 128 - width - target, 1)
                        )
                        fields[kind].at[c, plane_of(kind, p)][rows, pl.ds(0, 128)] = piece
            return carry

        lax.fori_loop(0, XROWS // 8, unpack_y, 0)

    def unpack_rows_x(planes, at, xrecv):
        def unpack_x(q, carry):
            p = at(q)
            for side in range(2):
                start = 0 if side == 0 else TOP + ROWS
                for group in range(3):
                    parts = xrecv[side, q, 8 * group:8 * group + 8, :]
                    parts = parts * (has_down if side == 0 else has_up)
                    for kind, c, width, place in PIECES[3 * group:3 * group + 3]:
                        target = place - 8 * group
                        shift = 8 - width - target if side == 0 else -target
                        fields[kind][c, plane_of(kind, p), start:start + 8, LEFT:XCOLS] = roll(
                            parts, shift, 0
                        )
            return carry

        lax.fori_loop(0, len(planes), unpack_x, 0)

    def ahead_x(tiles, t):
        here = tiles[t]
        if t < 9:
            here = jnp.where(sub3 == 0, tiles[t + 1], here)
        return pltpu.roll(here, 7, 0)

    def behind_x(tiles, t):
        here = tiles[t]
        if t > 0:
            here = jnp.where(sub3 == 7, tiles[t - 1], here)
        return pltpu.roll(here, 1, 0)

    def magnetic(start, stop):
        def one(p, carry):
            q = p + 1
            eys = {0: elec[1, p, 0:8, :]}
            ezs = {0: elec[2, p, 0:8, :]}
            for t in range(10):
                rows = slice(8 * t, 8 * t + 8)
                if t < 9:
                    eys[t + 1] = elec[1, p, 8 * t + 8:8 * t + 16, :]
                    ezs[t + 1] = elec[2, p, 8 * t + 8:8 * t + 16, :]
                ex, ey, ez = elec[0, p, rows, :], eys[t], ezs[t]
                factor = corner if t == 0 else half
                ez_y = pltpu.roll(ez, XCOLS - 1, 1)
                ex_y = pltpu.roll(ex, XCOLS - 1, 1)
                ez_x = ahead_x(ezs, t)
                ey_x = ahead_x(eys, t)
                magn[0, q, rows, :] -= factor * ((ez_y - ez) - (elec[1, q, rows, :] - ey))
                magn[1, q, rows, :] -= factor * ((elec[0, q, rows, :] - ex) - (ez_x - ez))
                magn[2, q, rows, :] -= factor * ((ey_x - ey) - (ex_y - ex))
            return carry

        lax.fori_loop(start, stop, one, 0)

    def electric(start, stop):
        def one(p, carry):
            q = p + 1
            hys, hzs = {}, {}
            for t in range(10):
                rows = slice(8 * t, 8 * t + 8)
                hys[t] = magn[1, q, rows, :]
                hzs[t] = magn[2, q, rows, :]
                hx, hy, hz = magn[0, q, rows, :], hys[t], hzs[t]
                hz_y = pltpu.roll(hz, 1, 1)
                hx_y = pltpu.roll(hx, 1, 1)
                hz_x = behind_x(hzs, t)
                hy_x = behind_x(hys, t)
                elec[0, p, rows, :] += (COURANT * perm[0, p, rows, :]) * (
                    (hz - hz_y) - (hy - magn[1, p, rows, :])
                )
                elec[1, p, rows, :] += (COURANT * perm[1, p, rows, :]) * (
                    (hx - magn[0, p, rows, :]) - (hz - hz_x)
                )
                elec[2, p, rows, :] += (COURANT * perm[2, p, rows, :]) * (
                    (hy - hy_x) - (hx - hx_y)
                )
            return carry

        lax.fori_loop(start, stop, one, 0)

    for copy in loads_i:
        copy.wait()
    inner_at = lambda q: q + 3
    outer_at = lambda q: q + 10 * (q // 3)
    copies_i = exchange(0, ysend_i, yrecv_i, xsend_i, xrecv_i)
    pack_rows_x(INNER, inner_at, xsend_i)
    pl.semaphore_wait(barrier, len(greeted))
    for copy in copies_i[:2]:
        copy.start()
    pack_rows_y(INNER, ysend_i)
    for copy in copies_i[2:]:
        copy.start()

    for copy in loads_t:
        copy.wait()

    for c in range(3):
        elec[c, NZ] = jnp.zeros((XROWS, XCOLS), F32)
        magn[c, 0] = jnp.zeros((XROWS, XCOLS), F32)

    place = lax.broadcasted_iota(jnp.int32, (16, 128), 0)
    angle = jnp.zeros((16, 128), F32)
    for f in range(FREQ):
        for s in range(3):
            angle = jnp.where(place == 3 * f + s, freq_in[f] * (s + 1.0), angle)
    both = (jnp.cos(angle), jnp.sin(angle))
    for f in range(FREQ):
        for s in range(3):
            k = 3 * f + s
            for part in range(2):
                trig[f, s, part] = jnp.broadcast_to(both[part][k:k + 1, :], (8, 128))

    col = gy * COLS + lax.broadcasted_iota(jnp.int32, (8, COLS), 1)
    inside = [
        ((col + b >= 0) & (col + b < n_y * COLS)).astype(F32) for b in range(-RADIUS, RADIUS + 1)
    ]
    sums = []
    for a in range(RADIUS + 1):
        total = jnp.zeros((8, COLS), F32)
        for b in range(-RADIUS, RADIUS + 1):
            if weight(a, b) > 0.0:
                total = total + weight(a, b) * inside[b + RADIUS]
        sums.append(total)

    def norm_tile(t, carry):
        row = gx * ROWS + t * 8 + sub
        total = jnp.zeros((8, COLS), F32)
        for a in range(-RADIUS, RADIUS + 1):
            within = ((row + a >= 0) & (row + a < n_x * ROWS)).astype(F32)
            total = total + within * sums[abs(a)]
        inverse_norm[tile_rows(t), :] = 1.0 / total
        return carry

    lax.fori_loop(0, ROWS // 8, norm_tile, 0)

    owners = owner_in[pl.ds(gx // 2, 1), :].astype(F32)
    lane1 = lax.broadcasted_iota(jnp.int32, (1, 128), 1)
    other = pltpu.roll(owners, 64, 1)
    low_half = lane1 < 64
    even = (lax.rem(gx, 2) == 0)
    keep = jnp.where(even, owners, other)
    swap = jnp.where(even, other, owners)
    owners = jnp.where(low_half, keep, pltpu.roll(keep, 64, 1))
    del swap
    rows_i = lax.broadcasted_iota(jnp.int32, (ROWS, 128), 0)
    lanes_j = lax.broadcasted_iota(jnp.int32, (ROWS, 128), 1)
    owners_b = jnp.broadcast_to(owners, (ROWS, 128))
    column = jnp.sum(jnp.where(rows_i == lanes_j, owners_b, 0.0), axis=1, keepdims=True)
    earlier = rows_i < jnp.where(lanes_j < 64, lanes_j, lanes_j - 64)
    same = jnp.where((column == owners_b) & earlier, 1.0, 0.0)
    slot = owners * CAP + jnp.sum(same, axis=0, keepdims=True)
    slots = jnp.concatenate([slot, slot], axis=1)
    wanted = lax.broadcasted_iota(jnp.int32, (n_x * CAP, 256), 0).astype(F32)
    used = lax.broadcasted_iota(jnp.int32, (n_x * CAP, 256), 1) < 3 * ROWS
    picker[...] = jnp.where((wanted == slots) & used, 1.0, 0.0).astype(jnp.bfloat16)

    for copy in loads_o:
        copy.wait()
    pack_rows_x(OUTER, outer_at, xsend_o)
    pack_rows_y(OUTER, ysend_o)
    for copy in copies_i[:2]:
        copy.wait()
    unpack_rows_x(INNER, inner_at, xrecv_i)
    for copy in copies_i[2:]:
        copy.wait()
    copies_o = exchange(1, ysend_o, yrecv_o, xsend_o, xrecv_o)
    for copy in copies_o:
        copy.start()
    unpack_rows_y(INNER, yrecv_i)

    for s in range(3):
        magnetic(3 + s, 12 - s)
        electric(4 + s, 12 - s)
        if s < 2:
            def keep_plane(p, carry, s=s):
                for c in range(3):
                    early[s, c, p] = elec[c, FIRST + p, TOP:TOP + ROWS, LEFT:XCOLS]
                return carry

            lax.fori_loop(0, DP, keep_plane, 0)

    for copy in loads_s:
        copy.wait()

    def gradient(k, carry):
        p, t = k // 8, lax.rem(k, 8)
        rows = tile_rows(t)
        ext = pl.ds(pl.multiple_of(TOP + t * 8, 8), 8)
        for h in range(2):
            cols = slice(128 * h, 128 * h + 128)
            far = slice(LEFT + 128 * h, LEFT + 128 * h + 128)
            fields_e = [
                [early[0, c, p, rows, cols], early[1, c, p, rows, cols], elec[c, FIRST + p, ext, far]]
                for c in range(3)
            ]
            keep = mask[p, rows, cols].astype(F32)
            for f in range(FREQ):
                total = jnp.zeros((8, 128), F32)
                for part in range(2):
                    w1, w2, w3 = (trig[f, s, part] for s in range(3))
                    for c in range(3):
                        e1, e2, e3 = fields_e[c]
                        total = total + spec[f, part, c, p, rows, cols] * (
                            w1 * e1 + w2 * e2 + w3 * e3
                        )
                masked[f * DP + p, ext, far] = total * keep
        return carry

    lax.fori_loop(0, DP * 8, gradient, 0)

    for t in range(ROWS // 8):
        ext = slice(TOP + t * 8, TOP + t * 8 + 8)
        for side in range(2):
            parts = jnp.zeros((8, 128), F32)
            for m in range(FREQ * DP):
                if side == 0:
                    piece = roll(masked[m, ext, 256:384], 3 * m + 3, 1)
                else:
                    piece = roll(masked[m, ext, 128:256], 3 * m, 1)
                parts = jnp.where(lane < 3 * m, parts, piece)
            ysend_m[side, 8 * t:8 * t + 8, :] = parts
    for j in range(FREQ * DP // 2):
        for side in range(2):
            start = TOP + ROWS - 8 if side == 0 else TOP
            first = masked[2 * j, start:start + 8, LEFT:XCOLS]
            second = pltpu.roll(masked[2 * j + 1, start:start + 8, LEFT:XCOLS], 3, 0)
            if side == 0:
                parts = jnp.where(sub < 3, second, first)
            else:
                parts = jnp.where(sub < 3, first, second)
            xsend_m[side, 8 * j:8 * j + 8, :] = parts
    copies_m = exchange(2, ysend_m, yrecv_m, xsend_m, xrecv_m)
    for copy in copies_m:
        copy.start()
    for copy in copies_m:
        copy.wait()

    def put_y(t, carry):
        rows = tile_rows(t)
        there = jnp.where(t == 0, has_down, jnp.where(t == 9, has_up, 1.0))
        low = yrecv_m[0, rows, :] * (there * has_left)
        high = yrecv_m[1, rows, :] * (there * has_right)
        for m in range(FREQ * DP):
            masked[m, rows, 0:128] = jnp.where(
                lane < 64, roll(high, -3 * m, 1), roll(low, 125 - 3 * m, 1)
            )
        return carry

    lax.fori_loop(0, XROWS // 8, put_y, 0)

    def put_x(j, carry):
        for side in range(2):
            start = 0 if side == 0 else TOP + ROWS
            parts = xrecv_m[side, tile_rows(j), :] * (has_down if side == 0 else has_up)
            masked[2 * j, start:start + 8, LEFT:XCOLS] = parts
            masked[2 * j + 1, start:start + 8, LEFT:XCOLS] = pltpu.roll(parts, 5, 0)
        return carry

    lax.fori_loop(0, FREQ * DP // 2, put_x, 0)

    routes = []
    for f in range(FREQ):
        def filter_plane(p, carry, f=f):
            m = f * DP + p
            for t in range(10):
                value = masked[m, 8 * t:8 * t + 8, :]
                center = value[:, LEFT:XCOLS]
                pairs = [
                    (pltpu.roll(value, b, 1) + pltpu.roll(value, XCOLS - b, 1))[:, LEFT:XCOLS]
                    for b in range(1, RADIUS + 1)
                ]
                for a in range(RADIUS + 1):
                    if a == 0 and t in (0, 9):
                        continue
                    total = weight(a, 0) * center
                    for b in range(1, RADIUS + 1):
                        if weight(a, b) > 0.0:
                            total = total + weight(a, b) * pairs[b - 1]
                    fold[a, 8 * t:8 * t + 8, :] = total
            for t in range(1, 9):
                total = fold[0, 8 * t:8 * t + 8, :]
                for a in range(1, RADIUS + 1):
                    here = fold[a, 8 * t:8 * t + 8, :]
                    after = fold[a, 8 * t + 8:8 * t + 16, :]
                    before = fold[a, 8 * t - 8:8 * t, :]
                    total = total + pltpu.roll(jnp.where(sub < a, after, here), 8 - a, 0)
                    total = total + pltpu.roll(jnp.where(sub >= 8 - a, before, here), a, 0)
                plane_out[8 * t - 8:8 * t, :] = total * inverse_norm[8 * t - 8:8 * t, :]
            value = plane_out[...]
            high = value.astype(jnp.bfloat16)
            rest = value - high.astype(F32)
            middle = rest.astype(jnp.bfloat16)
            low = (rest - middle.astype(F32)).astype(jnp.bfloat16)
            stacked = jnp.concatenate([high, middle, low, jnp.zeros_like(low)], axis=0)
            packed[f, p] = jnp.dot(picker[...], stacked, preferred_element_type=F32)
            return carry

        lax.fori_loop(0, DP, filter_plane, 0)
        mine = pl.ds(pl.multiple_of(gx * CAP, CAP), CAP)
        for k in list(range(n_x // 2, n_x)) + list(range(1, n_x // 2)):
            owner = gx ^ k
            theirs = pl.ds(pl.multiple_of(owner * CAP, CAP), CAP)
            copy = pltpu.make_async_remote_copy(
                src_ref=packed.at[f, :, theirs], dst_ref=owned_out.at[f, :, mine],
                send_sem=route_send.at[f, k], recv_sem=route_recv.at[f, k],
                device_id=(owner, gy), device_id_type=MESH,
            )
            copy.start()
            routes.append(copy)
        copy = pltpu.make_async_copy(packed.at[f, :, mine], owned_out.at[f, :, mine], own_sem.at[f])
        copy.start()
        routes.append(copy)

    for copy in copies_o:
        copy.wait()
    unpack_rows_x(OUTER, outer_at, xrecv_o)
    unpack_rows_y(OUTER, yrecv_o)
    for s in range(3):
        magnetic(12 - s, NZ)
        magnetic(0, 3 + s)
        electric(12 - s, NZ)
        electric(0, 4 + s)
    for copy in routes:
        copy.wait()


def save(elec, magn, owned, elec_out, magn_out, owned_out, sem):
    own_r, own_c = pl.ds(TOP, ROWS), pl.ds(LEFT, COLS)
    copies = [
        pltpu.make_async_copy(elec.at[:, pl.ds(0, NZ), own_r, own_c], elec_out, sem.at[0]),
        pltpu.make_async_copy(magn.at[:, pl.ds(1, NZ), own_r, own_c], magn_out, sem.at[1]),
        pltpu.make_async_copy(owned, owned_out, sem.at[2]),
    ]
    for copy in copies:
        copy.start()
    for copy in copies:
        copy.wait()


def body(n_x, n_y, elec, magn, perm, spec, freq, mask, owner):
    hbm = pl.BlockSpec(memory_space=pltpu.HBM)
    vmem = pl.BlockSpec(memory_space=pltpu.VMEM)
    buf = pltpu.VMEM
    sem = pltpu.SemaphoreType.DMA
    held = pl.pallas_call(
        functools.partial(kernel, n_x, n_y),
        out_shape=(
            buf((3, NZ + 1, XROWS, XCOLS), F32),
            buf((3, NZ + 1, XROWS, XCOLS), F32),
            buf((FREQ, DP, n_x * CAP, COLS), F32),
        ),
        in_specs=[hbm] * 7,
        out_specs=(vmem, vmem, vmem),
        scratch_shapes=[
            buf((3, NZ, XROWS, XCOLS), F32),
            buf((FREQ, 2, 3, DP, ROWS, COLS), F32),
            pltpu.SMEM((FREQ,), F32),
            buf((DP, ROWS, COLS), jnp.int32),
            buf((8, 128), jnp.int32),
            buf((FREQ, 3, 2, 8, 128), F32),
            buf((2, 3, DP, ROWS, COLS), F32),
            buf((FREQ * DP, XROWS, XCOLS), F32),
            buf((ROWS, COLS), F32),
            buf((n_x * CAP, 256), jnp.bfloat16),
            buf((RADIUS + 1, XROWS, COLS), F32),
            buf((ROWS, COLS), F32),
            buf((FREQ, DP, n_x * CAP, COLS), F32),
            buf((2, ROWS, 256), F32), buf((2, XROWS, 256), F32),
            buf((2, len(INNER), 24, COLS), F32), buf((2, len(INNER), 24, COLS), F32),
            buf((2, ROWS, 256), F32), buf((2, XROWS, 256), F32),
            buf((2, len(OUTER), 24, COLS), F32), buf((2, len(OUTER), 24, COLS), F32),
            buf((2, ROWS, 128), F32), buf((2, XROWS, 128), F32),
            buf((2, ROWS, COLS), F32), buf((2, ROWS, COLS), F32),
            sem((13,)), sem((FREQ,)), sem((3, 8)), sem((3, 8)),
            sem((FREQ, n_x)), sem((FREQ, n_x)),
        ],
        compiler_params=pltpu.CompilerParams(
            collective_id=0, has_side_effects=True, vmem_limit_bytes=36 << 20
        ),
        name="adjoint",
    )(*[pltpu.with_memory_space_constraint(v, pltpu.HBM) for v in (elec, magn, perm, spec, freq, mask, owner.reshape(8, 128))])
    return pl.pallas_call(
        save,
        out_shape=(
            jax.ShapeDtypeStruct((3, NZ, ROWS, COLS), F32),
            jax.ShapeDtypeStruct((3, NZ, ROWS, COLS), F32),
            jax.ShapeDtypeStruct((FREQ, DP, n_x * CAP, COLS), F32),
        ),
        in_specs=[vmem] * 3,
        out_specs=(hbm,) * 3,
        scratch_shapes=[sem((3,))],
        compiler_params=pltpu.CompilerParams(vmem_limit_bytes=1 << 20),
        name="save",
    )(*held)


def solution(mesh):
    placed = (
        P(None, None, "gx", "gy"),
        P(None, None, "gx", "gy"),
        P(None, None, "gx", "gy"),
        P(None, None, None, None, "gx", "gy"),
        P(),
        P(None, "gx", "gy"),
        P(),
    )
    return jax.shard_map(
        functools.partial(body, mesh.shape["gx"], mesh.shape["gy"]),
        mesh=mesh,
        in_specs=placed,
        out_specs=(P(None, None, "gx", "gy"), P(None, None, "gx", "gy"), P(None, None, "gx", "gy")),
        check_vma=False,
    )
```

```python
import functools
import math

import jax
import jax.numpy as jnp
from jax import lax
from jax.experimental import pallas as pl
from jax.experimental.pallas import tpu as pltpu
from jax.sharding import PartitionSpec as P

MESH = pl.DeviceIdType.MESH
F32 = jnp.float32

NZ = 16
ROWS = 64
COLS = 256
TOP = 8
LEFT = 128
XROWS = 80
XCOLS = 384
DP = 4
FIRST = 6
FREQ = 4
RADIUS = 3
CAP = 8
COURANT = 0.5

PIECES = (
    (0, 0, 3, 0), (0, 1, 3, 3), (2, 0, 2, 6),
    (0, 2, 3, 8), (1, 0, 3, 11), (2, 1, 2, 14),
    (1, 1, 3, 16), (1, 2, 3, 19), (2, 2, 2, 22),
)
INNER = tuple(range(3, 13))
OUTER = (0, 1, 2, 13, 14, 15)


def weight(shift_x, shift_y):
    return RADIUS + 1.0 - math.sqrt(shift_x * shift_x + shift_y * shift_y)


def roll(value, shift, axis):
    shift = shift % value.shape[axis]
    return value if shift == 0 else pltpu.roll(value, shift, axis)


def tile_rows(tile):
    return pl.ds(pl.multiple_of(tile * 8, 8), 8)


def kernel(
    n_x, n_y,
    elec_in, magn_in, perm_in, spec_in, freq_hbm, mask_in, owner_hbm,
    elec_out, magn_out, owned_out,
    elec, magn, perm, spec, freq_in, mask, owner_in, trig, early, masked, inverse_norm, picker,
    fold, plane_out, packed, landed,
    ysend_i, yrecv_i, xsend_i, xrecv_i,
    ysend_o, yrecv_o, xsend_o, xrecv_o,
    ysend_m, yrecv_m, xsend_m, xrecv_m,
    load_sem, save_sem, send_sem, recv_sem, route_sem,
):
    gx = lax.axis_index("gx")
    gy = lax.axis_index("gy")
    x_up, x_down = lax.rem(gx + 1, n_x), lax.rem(gx + n_x - 1, n_x)
    y_up, y_down = lax.rem(gy + 1, n_y), lax.rem(gy + n_y - 1, n_y)

    barrier = pltpu.get_barrier_semaphore()
    greeted = [(lax.rem(gx + k, n_x), gy) for k in range(1, n_x)]
    greeted += [(x, y) for x in (x_down, gx, x_up) for y in (y_down, y_up)]
    for peer in greeted:
        pl.semaphore_signal(barrier, inc=1, device_id=peer, device_id_type=MESH)

    own_r, own_c = pl.ds(TOP, ROWS), pl.ds(LEFT, COLS)

    def load(source, target, first, count, shift, sem):
        return pltpu.make_async_copy(
            source.at[:, pl.ds(first, count)],
            target.at[:, pl.ds(first + shift, count), own_r, own_c],
            load_sem.at[sem],
        )

    loads_i = [
        load(elec_in, elec, 3, 10, 0, 0),
        load(magn_in, magn, 3, 10, 1, 1),
        load(perm_in, perm, 3, 10, 0, 2),
    ]
    loads_o = [
        load(elec_in, elec, 0, 3, 0, 3), load(elec_in, elec, 13, 3, 0, 3),
        load(magn_in, magn, 0, 3, 1, 4), load(magn_in, magn, 13, 3, 1, 4),
        load(perm_in, perm, 0, 3, 0, 5), load(perm_in, perm, 13, 3, 0, 5),
    ]
    loads_s = [
        pltpu.make_async_copy(spec_in, spec, load_sem.at[6]),
        pltpu.make_async_copy(mask_in, mask, load_sem.at[7]),
    ]
    loads_t = [
        pltpu.make_async_copy(freq_hbm, freq_in, load_sem.at[8]),
        pltpu.make_async_copy(owner_hbm, owner_in, load_sem.at[9]),
    ]
    for copy in loads_t:
        copy.start()
    for copy in loads_i:
        copy.start()
    for copy in loads_o:
        copy.start()
    for copy in loads_s:
        copy.start()

    lane = lax.broadcasted_iota(jnp.int32, (8, 128), 1)
    lanes = lax.broadcasted_iota(jnp.int32, (8, XCOLS), 1)
    sub3 = lax.broadcasted_iota(jnp.int32, (8, XCOLS), 0)
    sub = lax.broadcasted_iota(jnp.int32, (8, COLS), 0)
    has_down = jnp.where(gx > 0, 1.0, 0.0).astype(F32)
    has_up = jnp.where(gx < n_x - 1, 1.0, 0.0).astype(F32)
    has_left = jnp.where(gy > 0, 1.0, 0.0).astype(F32)
    has_right = jnp.where(gy < n_y - 1, 1.0, 0.0).astype(F32)

    fields = (elec, magn, perm)

    half = jnp.where((lanes >= 64) & (lanes < 128), COURANT * has_left, COURANT)
    corner = half * has_down

    def plane_of(kind, p):
        return p + 1 if kind == 1 else p

    def pack_rows_y(planes, ysend):
        def pack_y(t, carry):
            rows = pl.ds(pl.multiple_of(TOP + t * 8, 8), 8)
            for side in range(2):
                for group in range(2):
                    parts = jnp.zeros((8, 128), F32)
                    for i, p in enumerate(planes[5 * group:5 * group + 5]):
                        for kind, c, width, place in PIECES:
                            target = 24 * i + place
                            ref = fields[kind].at[c, plane_of(kind, p)]
                            if side == 0:
                                piece = ref[rows, pl.ds(2 * 128, 128)]
                                piece = roll(piece, target - (128 - width), 1)
                            else:
                                piece = ref[rows, pl.ds(128, 128)]
                                piece = roll(piece, target, 1)
                            parts = jnp.where(lane < target, parts, piece)
                    ysend[side, tile_rows(t), group * 128:group * 128 + 128] = parts
            return carry

        lax.fori_loop(0, ROWS // 8, pack_y, 0)

    def pack_rows_x(planes, at, xsend):
        def pack_x(q, carry):
            p = at(q)
            for side in range(2):
                start = TOP + ROWS - 8 if side == 0 else TOP
                for group in range(3):
                    parts = None
                    for kind, c, width, place in PIECES[3 * group:3 * group + 3]:
                        target = place - 8 * group
                        piece = fields[kind][c, plane_of(kind, p), start:start + 8, LEFT:XCOLS]
                        piece = roll(piece, target - (8 - width) if side == 0 else target, 0)
                        parts = piece if parts is None else jnp.where(sub < target, parts, piece)
                    xsend[side, q, 8 * group:8 * group + 8, :] = parts
            return carry

        lax.fori_loop(0, len(planes), pack_x, 0)

    def exchange(stage, ysend, yrecv, xsend, xrecv, top, count):
        plan = [
            (xsend.at[0], xrecv.at[0], (x_up, gy)),
            (xsend.at[1], xrecv.at[1], (x_down, gy)),
        ]
        for side, y in ((0, y_up), (1, y_down)):
            plan += [
                (ysend.at[side], yrecv.at[side, pl.ds(top, count)], (gx, y)),
                (ysend.at[side, pl.ds(count - 8, 8)], yrecv.at[side, pl.ds(0, 8)], (x_up, y)),
                (ysend.at[side, pl.ds(0, 8)], yrecv.at[side, pl.ds(top + count, 8)], (x_down, y)),
            ]
        return [
            pltpu.make_async_remote_copy(
                src_ref=source, dst_ref=target,
                send_sem=send_sem.at[stage, min(i // 2, 1)],
                recv_sem=recv_sem.at[stage, min(i // 2, 1)],
                device_id=peer, device_id_type=MESH,
            )
            for i, (source, target, peer) in enumerate(plan)
        ]

    def finish(stage, kind, buffer):
        copy = pltpu.make_async_remote_copy(
            src_ref=buffer, dst_ref=buffer,
            send_sem=send_sem.at[stage, kind], recv_sem=recv_sem.at[stage, kind],
            device_id=(x_up, gy), device_id_type=MESH,
        )
        copy.wait()

    def unpack_rows_y(planes, yrecv):
        def unpack_y(t, carry):
            rows = tile_rows(t)
            there = jnp.where(t == 0, has_down, jnp.where(t == 9, has_up, 1.0))
            for group in range(2):
                if not planes[5 * group:5 * group + 5]:
                    continue
                cols = pl.ds(group * 128, 128)
                low = yrecv[0, rows, cols] * (there * has_left)
                high = yrecv[1, rows, cols] * (there * has_right)
                for i, p in enumerate(planes[5 * group:5 * group + 5]):
                    for kind, c, width, place in PIECES:
                        target = 24 * i + place
                        piece = jnp.where(
                            lane < 64, roll(high, -target, 1), roll(low, 128 - width - target, 1)
                        )
                        fields[kind].at[c, plane_of(kind, p)][rows, pl.ds(0, 128)] = piece
            return carry

        lax.fori_loop(0, XROWS // 8, unpack_y, 0)

    def unpack_rows_x(planes, at, xrecv):
        def unpack_x(q, carry):
            p = at(q)
            for side in range(2):
                start = 0 if side == 0 else TOP + ROWS
                for group in range(3):
                    parts = xrecv[side, q, 8 * group:8 * group + 8, :]
                    parts = parts * (has_down if side == 0 else has_up)
                    for kind, c, width, place in PIECES[3 * group:3 * group + 3]:
                        target = place - 8 * group
                        shift = 8 - width - target if side == 0 else -target
                        fields[kind][c, plane_of(kind, p), start:start + 8, LEFT:XCOLS] = roll(
                            parts, shift, 0
                        )
            return carry

        lax.fori_loop(0, len(planes), unpack_x, 0)

    def ahead_x(tiles, t):
        here = tiles[t]
        if t < 9:
            here = jnp.where(sub3 == 0, tiles[t + 1], here)
        return pltpu.roll(here, 7, 0)

    def behind_x(tiles, t):
        here = tiles[t]
        if t > 0:
            here = jnp.where(sub3 == 7, tiles[t - 1], here)
        return pltpu.roll(here, 1, 0)

    def magnetic(start, stop):
        def one(p, carry):
            q = p + 1
            eys = {0: elec[1, p, 0:8, :]}
            ezs = {0: elec[2, p, 0:8, :]}
            for t in range(10):
                rows = slice(8 * t, 8 * t + 8)
                if t < 9:
                    eys[t + 1] = elec[1, p, 8 * t + 8:8 * t + 16, :]
                    ezs[t + 1] = elec[2, p, 8 * t + 8:8 * t + 16, :]
                ex, ey, ez = elec[0, p, rows, :], eys[t], ezs[t]
                factor = corner if t == 0 else half
                ez_y = pltpu.roll(ez, XCOLS - 1, 1)
                ex_y = pltpu.roll(ex, XCOLS - 1, 1)
                ez_x = ahead_x(ezs, t)
                ey_x = ahead_x(eys, t)
                magn[0, q, rows, :] -= factor * ((ez_y - ez) - (elec[1, q, rows, :] - ey))
                magn[1, q, rows, :] -= factor * ((elec[0, q, rows, :] - ex) - (ez_x - ez))
                magn[2, q, rows, :] -= factor * ((ey_x - ey) - (ex_y - ex))
            return carry

        lax.fori_loop(start, stop, one, 0)

    def electric(start, stop):
        def one(p, carry):
            q = p + 1
            hys, hzs = {}, {}
            for t in range(10):
                rows = slice(8 * t, 8 * t + 8)
                hys[t] = magn[1, q, rows, :]
                hzs[t] = magn[2, q, rows, :]
                hx, hy, hz = magn[0, q, rows, :], hys[t], hzs[t]
                hz_y = pltpu.roll(hz, 1, 1)
                hx_y = pltpu.roll(hx, 1, 1)
                hz_x = behind_x(hzs, t)
                hy_x = behind_x(hys, t)
                elec[0, p, rows, :] += (COURANT * perm[0, p, rows, :]) * (
                    (hz - hz_y) - (hy - magn[1, p, rows, :])
                )
                elec[1, p, rows, :] += (COURANT * perm[1, p, rows, :]) * (
                    (hx - magn[0, p, rows, :]) - (hz - hz_x)
                )
                elec[2, p, rows, :] += (COURANT * perm[2, p, rows, :]) * (
                    (hy - hy_x) - (hx - hx_y)
                )
            return carry

        lax.fori_loop(start, stop, one, 0)

    for copy in loads_i:
        copy.wait()
    inner_at = lambda q: q + 3
    outer_at = lambda q: q + 10 * (q // 3)
    copies_i = exchange(0, ysend_i, yrecv_i, xsend_i, xrecv_i, TOP, ROWS)
    pack_rows_x(INNER, inner_at, xsend_i)
    pl.semaphore_wait(barrier, len(greeted))
    for copy in copies_i[:2]:
        copy.start()
    pack_rows_y(INNER, ysend_i)
    for copy in copies_i[2:]:
        copy.start()

    for copy in loads_t:
        copy.wait()

    for c in range(3):
        elec[c, NZ] = jnp.zeros((XROWS, XCOLS), F32)
        magn[c, 0] = jnp.zeros((XROWS, XCOLS), F32)

    place = lax.broadcasted_iota(jnp.int32, (16, 128), 0)
    angle = jnp.zeros((16, 128), F32)
    for f in range(FREQ):
        for s in range(3):
            angle = jnp.where(place == 3 * f + s, freq_in[f] * (s + 1.0), angle)
    both = (jnp.cos(angle), jnp.sin(angle))
    for f in range(FREQ):
        for s in range(3):
            k = 3 * f + s
            for part in range(2):
                trig[f, s, part] = jnp.broadcast_to(both[part][k:k + 1, :], (8, 128))

    col = gy * COLS + lax.broadcasted_iota(jnp.int32, (8, COLS), 1)
    inside = [
        ((col + b >= 0) & (col + b < n_y * COLS)).astype(F32) for b in range(-RADIUS, RADIUS + 1)
    ]
    sums = []
    for a in range(RADIUS + 1):
        total = jnp.zeros((8, COLS), F32)
        for b in range(-RADIUS, RADIUS + 1):
            if weight(a, b) > 0.0:
                total = total + weight(a, b) * inside[b + RADIUS]
        sums.append(total)

    def norm_tile(t, carry):
        row = gx * ROWS + t * 8 + sub
        total = jnp.zeros((8, COLS), F32)
        for a in range(-RADIUS, RADIUS + 1):
            within = ((row + a >= 0) & (row + a < n_x * ROWS)).astype(F32)
            total = total + within * sums[abs(a)]
        inverse_norm[tile_rows(t), :] = 1.0 / total
        return carry

    lax.fori_loop(0, ROWS // 8, norm_tile, 0)

    owners = owner_in[pl.ds(gx // 2, 1), :].astype(F32)
    lane1 = lax.broadcasted_iota(jnp.int32, (1, 128), 1)
    other = pltpu.roll(owners, 64, 1)
    low_half = lane1 < 64
    even = (lax.rem(gx, 2) == 0)
    keep = jnp.where(even, owners, other)
    swap = jnp.where(even, other, owners)
    owners = jnp.where(low_half, keep, pltpu.roll(keep, 64, 1))
    del swap
    rows_i = lax.broadcasted_iota(jnp.int32, (ROWS, 128), 0)
    lanes_j = lax.broadcasted_iota(jnp.int32, (ROWS, 128), 1)
    owners_b = jnp.broadcast_to(owners, (ROWS, 128))
    column = jnp.sum(jnp.where(rows_i == lanes_j, owners_b, 0.0), axis=1, keepdims=True)
    earlier = rows_i < jnp.where(lanes_j < 64, lanes_j, lanes_j - 64)
    same = jnp.where((column == owners_b) & earlier, 1.0, 0.0)
    slot = owners * CAP + jnp.sum(same, axis=0, keepdims=True)
    slots = jnp.concatenate([slot, slot], axis=1)
    wanted = lax.broadcasted_iota(jnp.int32, (n_x * CAP, 256), 0).astype(F32)
    used = lax.broadcasted_iota(jnp.int32, (n_x * CAP, 256), 1) < 3 * ROWS
    picker[...] = jnp.where((wanted == slots) & used, 1.0, 0.0).astype(jnp.bfloat16)

    for k, (source, target) in enumerate(((elec_in, elec), (magn_in, magn), (perm_in, perm))):
        load(source, target, 0, 6, 0, 3 + k).wait()
    pack_rows_x(OUTER, outer_at, xsend_o)
    pack_rows_y(OUTER, ysend_o)
    finish(0, 0, xrecv_i)
    unpack_rows_x(INNER, inner_at, xrecv_i)
    finish(0, 1, yrecv_i)
    copies_o = exchange(1, ysend_o, yrecv_o, xsend_o, xrecv_o, TOP, ROWS)
    for copy in copies_o:
        copy.start()
    unpack_rows_y(INNER, yrecv_i)

    def keep_planes(s, start, stop):
        def keep_plane(p, carry):
            for c in range(3):
                early[s, c, p] = elec[c, FIRST + p, TOP:TOP + ROWS, LEFT:XCOLS]
            return carry

        lax.fori_loop(start, stop, keep_plane, 0)

    def gradient(k, carry):
        p, t = k // 8, lax.rem(k, 8)
        rows = tile_rows(t)
        ext = pl.ds(pl.multiple_of(TOP + t * 8, 8), 8)
        for h in range(2):
            cols = slice(128 * h, 128 * h + 128)
            far = slice(LEFT + 128 * h, LEFT + 128 * h + 128)
            fields_e = [
                [early[0, c, p, rows, cols], early[1, c, p, rows, cols], elec[c, FIRST + p, ext, far]]
                for c in range(3)
            ]
            keep = mask[p, rows, cols].astype(F32)
            for f in range(FREQ):
                total = jnp.zeros((8, 128), F32)
                for part in range(2):
                    w1, w2, w3 = (trig[f, s, part] for s in range(3))
                    for c in range(3):
                        e1, e2, e3 = fields_e[c]
                        total = total + spec[f, part, c, p, rows, cols] * (
                            w1 * e1 + w2 * e2 + w3 * e3
                        )
                masked[p * FREQ + f, ext, far] = total * keep
        return carry

    def send_edges(part):
        lax.fori_loop(part * 16, part * 16 + 16, gradient, 0)
        for side in range(2):
            for odd in range(2):
                parts = jnp.zeros((8, 128), F32)
                for group in range(4):
                    t = 2 * group + odd
                    ext = slice(TOP + t * 8, TOP + t * 8 + 8)
                    for q in range(8):
                        m, target = part * 8 + q, 32 * group + 3 * q
                        if side == 0:
                            piece = roll(masked[m, ext, 256:384], target + 3, 1)
                        else:
                            piece = roll(masked[m, ext, 128:256], target, 1)
                        parts = jnp.where(lane < target, parts, piece)
                ysend_m[part, side, 8 * odd:8 * odd + 8, :] = parts
            for j in range(4):
                start = TOP + ROWS - 8 if side == 0 else TOP
                m = part * 8 + 2 * j
                first = masked[m, start:start + 8, LEFT:XCOLS]
                second = pltpu.roll(masked[m + 1, start:start + 8, LEFT:XCOLS], 3, 0)
                if side == 0:
                    parts = jnp.where(sub < 3, second, first)
                else:
                    parts = jnp.where(sub < 3, first, second)
                xsend_m[part, side, 8 * j:8 * j + 8, :] = parts
        for copy in exchange(
            2 + part, ysend_m.at[part], yrecv_m.at[part], xsend_m.at[part], xrecv_m.at[part], 8, 16
        ):
            copy.start()

    def put_edges(part):
        finish(2 + part, 0, xrecv_m.at[part])
        for side in range(2):
            start = 0 if side == 0 else TOP + ROWS
            for j in range(4):
                m = part * 8 + 2 * j
                parts = xrecv_m[part, side, 8 * j:8 * j + 8, :]
                parts = parts * (has_down if side == 0 else has_up)
                masked[m, start:start + 8, LEFT:XCOLS] = parts
                masked[m + 1, start:start + 8, LEFT:XCOLS] = pltpu.roll(parts, 5, 0)
        finish(2 + part, 1, yrecv_m.at[part])
        for t in range(10):
            if t == 0:
                there, row, shift = has_down, 0, 96
            elif t == 9:
                there, row, shift = has_up, 24, 0
            else:
                there, row, shift = 1.0, 8 + 8 * ((t - 1) % 2), 32 * ((t - 1) // 2)
            low = yrecv_m[part, 0, row:row + 8, :] * (there * has_left)
            high = yrecv_m[part, 1, row:row + 8, :] * (there * has_right)
            for q in range(8):
                target = shift + 3 * q
                masked[part * 8 + q, 8 * t:8 * t + 8, 0:128] = jnp.where(
                    lane < 64, roll(high, -target, 1), roll(low, 125 - target, 1)
                )

    magnetic(3, 10)
    electric(4, 10)
    keep_planes(0, 0, DP)
    magnetic(4, 9)
    electric(5, 9)
    keep_planes(1, 0, 3)
    magnetic(5, 8)
    electric(6, 8)
    for copy in loads_s:
        copy.wait()
    send_edges(0)
    magnetic(10, 12)
    electric(10, 12)
    magnetic(9, 11)
    electric(9, 11)
    keep_planes(1, 3, DP)
    magnetic(8, 10)
    electric(8, 10)
    send_edges(1)

    def filter_plane(m, carry):
        for t in range(10):
            value = masked[m, 8 * t:8 * t + 8, :]
            center = value[:, LEFT:XCOLS]
            pairs = [
                (pltpu.roll(value, b, 1) + pltpu.roll(value, XCOLS - b, 1))[:, LEFT:XCOLS]
                for b in range(1, RADIUS + 1)
            ]
            for a in range(RADIUS + 1):
                if a == 0 and t in (0, 9):
                    continue
                total = weight(a, 0) * center
                for b in range(1, RADIUS + 1):
                    if weight(a, b) > 0.0:
                        total = total + weight(a, b) * pairs[b - 1]
                fold[a, 8 * t:8 * t + 8, :] = total
        for t in range(1, 9):
            total = fold[0, 8 * t:8 * t + 8, :]
            for a in range(1, RADIUS + 1):
                here = fold[a, 8 * t:8 * t + 8, :]
                after = fold[a, 8 * t + 8:8 * t + 16, :]
                before = fold[a, 8 * t - 8:8 * t, :]
                total = total + pltpu.roll(jnp.where(sub < a, after, here), 8 - a, 0)
                total = total + pltpu.roll(jnp.where(sub >= 8 - a, before, here), a, 0)
            plane_out[8 * t - 8:8 * t, :] = total * inverse_norm[8 * t - 8:8 * t, :]
        value = plane_out[...]
        high = value.astype(jnp.bfloat16)
        rest = value - high.astype(F32)
        middle = rest.astype(jnp.bfloat16)
        low = (rest - middle.astype(F32)).astype(jnp.bfloat16)
        stacked = jnp.concatenate([high, middle, low, jnp.zeros_like(low)], axis=0)
        picked = jnp.dot(picker[...], stacked, preferred_element_type=F32)
        packed[lax.rem(m, FREQ), m // FREQ] = picked
        return carry

    mine = pl.ds(pl.multiple_of(gx * CAP, CAP), CAP)
    for p in range(DP):
        if p % 2 == 0:
            put_edges(p // 2)
        lax.fori_loop(p * FREQ, p * FREQ + FREQ, filter_plane, 0)
        for k in list(range(n_x // 2, n_x)) + list(range(1, n_x // 2)):
            owner = gx ^ k
            theirs = pl.ds(pl.multiple_of(owner * CAP, CAP), CAP)
            pltpu.make_async_remote_copy(
                src_ref=packed.at[:, p, theirs], dst_ref=landed.at[:, p, mine],
                send_sem=route_sem.at[0], recv_sem=route_sem.at[1],
                device_id=(owner, gy), device_id_type=MESH,
            ).start()
        pltpu.make_async_copy(
            packed.at[:, p, mine], landed.at[:, p, mine], route_sem.at[2]
        ).start()

    finish(1, 0, xrecv_o)
    finish(1, 1, yrecv_o)
    unpack_rows_x(OUTER, outer_at, xrecv_o)
    unpack_rows_y(OUTER, yrecv_o)
    for s in range(3):
        magnetic(12 - s, NZ)
        magnetic(0, 3 + s)
        electric(12 - s, NZ)
        electric(0, 4 + s)
    saves = [
        pltpu.make_async_copy(elec.at[:, pl.ds(0, NZ), own_r, own_c], elec_out, save_sem.at[0]),
        pltpu.make_async_copy(magn.at[:, pl.ds(1, NZ), own_r, own_c], magn_out, save_sem.at[1]),
    ]
    for copy in saves:
        copy.start()
    for copy in saves:
        copy.wait()
    others = pl.ds(0, (n_x - 1) * CAP)
    pltpu.make_async_remote_copy(
        src_ref=packed.at[:, :, others], dst_ref=landed.at[:, :, others],
        send_sem=route_sem.at[0], recv_sem=route_sem.at[1],
        device_id=(x_up, gy), device_id_type=MESH,
    ).wait()
    first = pl.ds(0, CAP)
    pltpu.make_async_copy(packed.at[:, :, first], landed.at[:, :, first], route_sem.at[2]).wait()
    copy = pltpu.make_async_copy(landed, owned_out, save_sem.at[2])
    copy.start()
    copy.wait()


def save(elec, magn, owned, elec_out, magn_out, owned_out, sem):
    copies = [
        pltpu.make_async_copy(elec, elec_out, sem.at[0]),
        pltpu.make_async_copy(magn, magn_out, sem.at[1]),
        pltpu.make_async_copy(owned, owned_out, sem.at[2]),
    ]
    for copy in copies:
        copy.start()
    for copy in copies:
        copy.wait()


def body(n_x, n_y, elec, magn, perm, spec, freq, mask, owner):
    hbm = pl.BlockSpec(memory_space=pltpu.HBM)
    vmem = pl.BlockSpec(memory_space=pltpu.VMEM)
    any_space = pl.BlockSpec(memory_space=pl.ANY)
    buf = pltpu.VMEM
    sem = pltpu.SemaphoreType.DMA
    held = pl.pallas_call(
        functools.partial(kernel, n_x, n_y),
        out_shape=(
            buf((3, NZ, ROWS, COLS), F32),
            buf((3, NZ, ROWS, COLS), F32),
            buf((FREQ, DP, n_x * CAP, COLS), F32),
        ),
        in_specs=[hbm] * 7,
        out_specs=(any_space,) * 3,
        scratch_shapes=[
            buf((3, NZ + 1, XROWS, XCOLS), F32),
            buf((3, NZ + 1, XROWS, XCOLS), F32),
            buf((3, NZ, XROWS, XCOLS), F32),
            buf((FREQ, 2, 3, DP, ROWS, COLS), F32),
            pltpu.SMEM((FREQ,), F32),
            buf((DP, ROWS, COLS), jnp.int32),
            buf((8, 128), jnp.int32),
            buf((FREQ, 3, 2, 8, 128), F32),
            buf((2, 3, DP, ROWS, COLS), F32),
            buf((FREQ * DP, XROWS, XCOLS), F32),
            buf((ROWS, COLS), F32),
            buf((n_x * CAP, 256), jnp.bfloat16),
            buf((RADIUS + 1, XROWS, COLS), F32),
            buf((ROWS, COLS), F32),
            buf((FREQ, DP, n_x * CAP, COLS), F32),
            buf((FREQ, DP, n_x * CAP, COLS), F32),
            buf((2, ROWS, 256), F32), buf((2, XROWS, 256), F32),
            buf((2, len(INNER), 24, COLS), F32), buf((2, len(INNER), 24, COLS), F32),
            buf((2, ROWS, 256), F32), buf((2, XROWS, 256), F32),
            buf((2, len(OUTER), 24, COLS), F32), buf((2, len(OUTER), 24, COLS), F32),
            buf((2, 2, 16, 128), F32), buf((2, 2, 32, 128), F32),
            buf((2, 2, 32, COLS), F32), buf((2, 2, 32, COLS), F32),
            sem((10,)), sem((3,)), sem((4, 2)), sem((4, 2)), sem((3,)),
        ],
        compiler_params=pltpu.CompilerParams(
            collective_id=0, has_side_effects=True, vmem_limit_bytes=40 << 20
        ),
        name="adjoint",
    )(*[pltpu.with_memory_space_constraint(v, pltpu.HBM) for v in (elec, magn, perm, spec, freq, mask, owner.reshape(8, 128))])
    return pl.pallas_call(
        save,
        out_shape=(
            jax.ShapeDtypeStruct((3, NZ, ROWS, COLS), F32),
            jax.ShapeDtypeStruct((3, NZ, ROWS, COLS), F32),
            jax.ShapeDtypeStruct((FREQ, DP, n_x * CAP, COLS), F32),
        ),
        in_specs=[vmem] * 3,
        out_specs=(hbm,) * 3,
        scratch_shapes=[sem((3,))],
        compiler_params=pltpu.CompilerParams(vmem_limit_bytes=1 << 20),
        name="save",
    )(*held)


def solution(mesh):
    placed = (
        P(None, None, "gx", "gy"),
        P(None, None, "gx", "gy"),
        P(None, None, "gx", "gy"),
        P(None, None, None, None, "gx", "gy"),
        P(),
        P(None, "gx", "gy"),
        P(),
    )
    return jax.shard_map(
        functools.partial(body, mesh.shape["gx"], mesh.shape["gy"]),
        mesh=mesh,
        in_specs=placed,
        out_specs=(P(None, None, "gx", "gy"), P(None, None, "gx", "gy"), P(None, None, "gx", "gy")),
        check_vma=False,
    )
```

```python
import functools
import math

import jax
import jax.numpy as jnp
from jax import lax
from jax.experimental import pallas as pl
from jax.experimental.pallas import tpu as pltpu
from jax.sharding import PartitionSpec as P

MESH = pl.DeviceIdType.MESH
F32 = jnp.float32

NZ = 16
ROWS = 64
COLS = 256
TOP = 8
LEFT = 128
XROWS = 80
XCOLS = 384
DP = 4
FIRST = 6
FREQ = 4
RADIUS = 3
CAP = 8
COURANT = 0.5

PIECES = (
    (0, 0, 3, 0), (0, 1, 3, 3), (2, 0, 2, 6),
    (0, 2, 3, 8), (1, 0, 3, 11), (2, 1, 2, 14),
    (1, 1, 3, 16), (1, 2, 3, 19), (2, 2, 2, 22),
)
INNER = tuple(range(3, 13))
OUTER = (0, 1, 2, 13, 14, 15)


def weight(shift_x, shift_y):
    return RADIUS + 1.0 - math.sqrt(shift_x * shift_x + shift_y * shift_y)


def roll(value, shift, axis):
    shift = shift % value.shape[axis]
    return value if shift == 0 else pltpu.roll(value, shift, axis)


def tile_rows(tile):
    return pl.ds(pl.multiple_of(tile * 8, 8), 8)


def kernel(
    n_x, n_y,
    elec_in, magn_in, perm_in, spec_in, freq_hbm, mask_in, owner_hbm,
    elec_out, magn_out, owned_out,
    elec, magn, perm, spec, freq_in, mask, owner_in, trig, early, masked, inverse_norm, picker,
    fold, plane_out, packed,
    ysend_i, yrecv_i, xsend_i, xrecv_i,
    ysend_o, yrecv_o, xsend_o, xrecv_o,
    ysend_m, yrecv_m, xsend_m, xrecv_m,
    load_sem, save_sem, send_sem, recv_sem, route_sem,
):
    gx = lax.axis_index("gx")
    gy = lax.axis_index("gy")
    x_up, x_down = lax.rem(gx + 1, n_x), lax.rem(gx + n_x - 1, n_x)
    y_up, y_down = lax.rem(gy + 1, n_y), lax.rem(gy + n_y - 1, n_y)

    barrier = pltpu.get_barrier_semaphore()
    greeted = [(lax.rem(gx + k, n_x), gy) for k in range(1, n_x)]
    greeted += [(x, y) for x in (x_down, gx, x_up) for y in (y_down, y_up)]
    for peer in greeted:
        pl.semaphore_signal(barrier, inc=1, device_id=peer, device_id_type=MESH)

    own_r, own_c = pl.ds(TOP, ROWS), pl.ds(LEFT, COLS)

    def load(source, target, first, count, shift, sem):
        return pltpu.make_async_copy(
            source.at[:, pl.ds(first, count)],
            target.at[:, pl.ds(first + shift, count), own_r, own_c],
            load_sem.at[sem],
        )

    loads_i = [
        load(elec_in, elec, 3, 10, 0, 0),
        load(magn_in, magn, 3, 10, 1, 1),
        load(perm_in, perm, 3, 10, 0, 2),
    ]
    loads_o = [
        load(elec_in, elec, 0, 3, 0, 3), load(elec_in, elec, 13, 3, 0, 3),
        load(magn_in, magn, 0, 3, 1, 4), load(magn_in, magn, 13, 3, 1, 4),
        load(perm_in, perm, 0, 3, 0, 5), load(perm_in, perm, 13, 3, 0, 5),
    ]
    loads_s = [
        pltpu.make_async_copy(spec_in, spec, load_sem.at[6]),
        pltpu.make_async_copy(mask_in, mask, load_sem.at[7]),
    ]
    loads_t = [
        pltpu.make_async_copy(freq_hbm, freq_in, load_sem.at[8]),
        pltpu.make_async_copy(owner_hbm, owner_in, load_sem.at[9]),
    ]
    for copy in loads_t:
        copy.start()
    for copy in loads_i:
        copy.start()
    for copy in loads_o:
        copy.start()
    for copy in loads_s:
        copy.start()

    lane = lax.broadcasted_iota(jnp.int32, (8, 128), 1)
    lanes = lax.broadcasted_iota(jnp.int32, (8, XCOLS), 1)
    sub3 = lax.broadcasted_iota(jnp.int32, (8, XCOLS), 0)
    sub = lax.broadcasted_iota(jnp.int32, (8, COLS), 0)
    has_down = jnp.where(gx > 0, 1.0, 0.0).astype(F32)
    has_up = jnp.where(gx < n_x - 1, 1.0, 0.0).astype(F32)
    has_left = jnp.where(gy > 0, 1.0, 0.0).astype(F32)
    has_right = jnp.where(gy < n_y - 1, 1.0, 0.0).astype(F32)

    fields = (elec, magn, perm)

    half = jnp.where((lanes >= 64) & (lanes < 128), COURANT * has_left, COURANT)
    corner = half * has_down

    def plane_of(kind, p):
        return p + 1 if kind == 1 else p

    def pack_rows_y(planes, ysend):
        def pack_y(t, carry):
            rows = pl.ds(pl.multiple_of(TOP + t * 8, 8), 8)
            for side in range(2):
                for group in range(2):
                    parts = jnp.zeros((8, 128), F32)
                    for i, p in enumerate(planes[5 * group:5 * group + 5]):
                        for kind, c, width, place in PIECES:
                            target = 24 * i + place
                            ref = fields[kind].at[c, plane_of(kind, p)]
                            if side == 0:
                                piece = ref[rows, pl.ds(2 * 128, 128)]
                                piece = roll(piece, target - (128 - width), 1)
                            else:
                                piece = ref[rows, pl.ds(128, 128)]
                                piece = roll(piece, target, 1)
                            parts = jnp.where(lane < target, parts, piece)
                    ysend[side, tile_rows(t), group * 128:group * 128 + 128] = parts
            return carry

        lax.fori_loop(0, ROWS // 8, pack_y, 0)

    def pack_rows_x(planes, at, xsend):
        def pack_x(q, carry):
            p = at(q)
            for side in range(2):
                start = TOP + ROWS - 8 if side == 0 else TOP
                for group in range(3):
                    parts = None
                    for kind, c, width, place in PIECES[3 * group:3 * group + 3]:
                        target = place - 8 * group
                        piece = fields[kind][c, plane_of(kind, p), start:start + 8, LEFT:XCOLS]
                        piece = roll(piece, target - (8 - width) if side == 0 else target, 0)
                        parts = piece if parts is None else jnp.where(sub < target, parts, piece)
                    xsend[side, q, 8 * group:8 * group + 8, :] = parts
            return carry

        lax.fori_loop(0, len(planes), pack_x, 0)

    def exchange(stage, ysend, yrecv, xsend, xrecv, top, count):
        plan = [
            (xsend.at[0], xrecv.at[0], (x_up, gy)),
            (xsend.at[1], xrecv.at[1], (x_down, gy)),
        ]
        for side, y in ((0, y_up), (1, y_down)):
            plan += [
                (ysend.at[side], yrecv.at[side, pl.ds(top, count)], (gx, y)),
                (ysend.at[side, pl.ds(count - 8, 8)], yrecv.at[side, pl.ds(0, 8)], (x_up, y)),
                (ysend.at[side, pl.ds(0, 8)], yrecv.at[side, pl.ds(top + count, 8)], (x_down, y)),
            ]
        return [
            pltpu.make_async_remote_copy(
                src_ref=source, dst_ref=target,
                send_sem=send_sem.at[stage, min(i // 2, 1)],
                recv_sem=recv_sem.at[stage, min(i // 2, 1)],
                device_id=peer, device_id_type=MESH,
            )
            for i, (source, target, peer) in enumerate(plan)
        ]

    def finish(stage, kind, buffer):
        copy = pltpu.make_async_remote_copy(
            src_ref=buffer, dst_ref=buffer,
            send_sem=send_sem.at[stage, kind], recv_sem=recv_sem.at[stage, kind],
            device_id=(x_up, gy), device_id_type=MESH,
        )
        copy.wait()

    def unpack_rows_y(planes, yrecv, wanted):
        def unpack_y(t, carry):
            rows = tile_rows(t)
            there = jnp.where(t == 0, has_down, jnp.where(t == 9, has_up, 1.0))
            for group in range(2):
                if not set(planes[5 * group:5 * group + 5]) & set(wanted):
                    continue
                cols = pl.ds(group * 128, 128)
                low = yrecv[0, rows, cols] * (there * has_left)
                high = yrecv[1, rows, cols] * (there * has_right)
                for i, p in enumerate(planes[5 * group:5 * group + 5]):
                    if p not in wanted:
                        continue
                    for kind, c, width, place in PIECES:
                        target = 24 * i + place
                        piece = jnp.where(
                            lane < 64, roll(high, -target, 1), roll(low, 128 - width - target, 1)
                        )
                        fields[kind].at[c, plane_of(kind, p)][rows, pl.ds(0, 128)] = piece
            return carry

        lax.fori_loop(0, XROWS // 8, unpack_y, 0)

    def unpack_rows_x(start_q, stop_q, at, xrecv):
        def unpack_x(q, carry):
            p = at(q)
            for side in range(2):
                start = 0 if side == 0 else TOP + ROWS
                for group in range(3):
                    parts = xrecv[side, q, 8 * group:8 * group + 8, :]
                    parts = parts * (has_down if side == 0 else has_up)
                    for kind, c, width, place in PIECES[3 * group:3 * group + 3]:
                        target = place - 8 * group
                        shift = 8 - width - target if side == 0 else -target
                        fields[kind][c, plane_of(kind, p), start:start + 8, LEFT:XCOLS] = roll(
                            parts, shift, 0
                        )
            return carry

        lax.fori_loop(start_q, stop_q, unpack_x, 0)

    def ahead_x(tiles, t):
        here = tiles[t]
        if t < 9:
            here = jnp.where(sub3 == 0, tiles[t + 1], here)
        return pltpu.roll(here, 7, 0)

    def behind_x(tiles, t):
        here = tiles[t]
        if t > 0:
            here = jnp.where(sub3 == 7, tiles[t - 1], here)
        return pltpu.roll(here, 1, 0)

    def magnetic(start, stop):
        def one(p, carry):
            q = p + 1
            eys = {0: elec[1, p, 0:8, :]}
            ezs = {0: elec[2, p, 0:8, :]}
            for t in range(10):
                rows = slice(8 * t, 8 * t + 8)
                if t < 9:
                    eys[t + 1] = elec[1, p, 8 * t + 8:8 * t + 16, :]
                    ezs[t + 1] = elec[2, p, 8 * t + 8:8 * t + 16, :]
                ex, ey, ez = elec[0, p, rows, :], eys[t], ezs[t]
                factor = corner if t == 0 else half
                ez_y = pltpu.roll(ez, XCOLS - 1, 1)
                ex_y = pltpu.roll(ex, XCOLS - 1, 1)
                ez_x = ahead_x(ezs, t)
                ey_x = ahead_x(eys, t)
                magn[0, q, rows, :] -= factor * ((ez_y - ez) - (elec[1, q, rows, :] - ey))
                magn[1, q, rows, :] -= factor * ((elec[0, q, rows, :] - ex) - (ez_x - ez))
                magn[2, q, rows, :] -= factor * ((ey_x - ey) - (ex_y - ex))
            return carry

        lax.fori_loop(start, stop, one, 0)

    def electric(start, stop):
        def one(p, carry):
            q = p + 1
            hys, hzs = {}, {}
            for t in range(10):
                rows = slice(8 * t, 8 * t + 8)
                hys[t] = magn[1, q, rows, :]
                hzs[t] = magn[2, q, rows, :]
                hx, hy, hz = magn[0, q, rows, :], hys[t], hzs[t]
                hz_y = pltpu.roll(hz, 1, 1)
                hx_y = pltpu.roll(hx, 1, 1)
                hz_x = behind_x(hzs, t)
                hy_x = behind_x(hys, t)
                elec[0, p, rows, :] += (COURANT * perm[0, p, rows, :]) * (
                    (hz - hz_y) - (hy - magn[1, p, rows, :])
                )
                elec[1, p, rows, :] += (COURANT * perm[1, p, rows, :]) * (
                    (hx - magn[0, p, rows, :]) - (hz - hz_x)
                )
                elec[2, p, rows, :] += (COURANT * perm[2, p, rows, :]) * (
                    (hy - hy_x) - (hx - hx_y)
                )
            return carry

        lax.fori_loop(start, stop, one, 0)

    for copy in loads_i:
        copy.wait()
    inner_at = lambda q: q + 3
    outer_at = lambda q: q + 10 * (q // 3)
    copies_i = exchange(0, ysend_i, yrecv_i, xsend_i, xrecv_i, TOP, ROWS)
    pack_rows_x(INNER, inner_at, xsend_i)
    pl.semaphore_wait(barrier, len(greeted))
    for copy in copies_i[:2]:
        copy.start()
    pack_rows_y(INNER, ysend_i)
    for copy in copies_i[2:]:
        copy.start()

    for copy in loads_t:
        copy.wait()

    for c in range(3):
        elec[c, NZ] = jnp.zeros((XROWS, XCOLS), F32)
        magn[c, 0] = jnp.zeros((XROWS, XCOLS), F32)

    place = lax.broadcasted_iota(jnp.int32, (16, 128), 0)
    angle = jnp.zeros((16, 128), F32)
    for f in range(FREQ):
        for s in range(3):
            angle = jnp.where(place == 3 * f + s, freq_in[f] * (s + 1.0), angle)
    both = (jnp.cos(angle), jnp.sin(angle))
    for f in range(FREQ):
        for s in range(3):
            k = 3 * f + s
            for part in range(2):
                trig[f, s, part] = jnp.broadcast_to(both[part][k:k + 1, :], (8, 128))

    col = gy * COLS + lax.broadcasted_iota(jnp.int32, (8, COLS), 1)
    inside = [
        ((col + b >= 0) & (col + b < n_y * COLS)).astype(F32) for b in range(-RADIUS, RADIUS + 1)
    ]
    sums = []
    for a in range(RADIUS + 1):
        total = jnp.zeros((8, COLS), F32)
        for b in range(-RADIUS, RADIUS + 1):
            if weight(a, b) > 0.0:
                total = total + weight(a, b) * inside[b + RADIUS]
        sums.append(total)

    def norm_tile(t, carry):
        row = gx * ROWS + t * 8 + sub
        total = jnp.zeros((8, COLS), F32)
        for a in range(-RADIUS, RADIUS + 1):
            within = ((row + a >= 0) & (row + a < n_x * ROWS)).astype(F32)
            total = total + within * sums[abs(a)]
        inverse_norm[tile_rows(t), :] = 1.0 / total
        return carry

    lax.fori_loop(0, ROWS // 8, norm_tile, 0)

    owners = owner_in[pl.ds(gx // 2, 1), :].astype(F32)
    lane1 = lax.broadcasted_iota(jnp.int32, (1, 128), 1)
    other = pltpu.roll(owners, 64, 1)
    low_half = lane1 < 64
    even = (lax.rem(gx, 2) == 0)
    keep = jnp.where(even, owners, other)
    swap = jnp.where(even, other, owners)
    owners = jnp.where(low_half, keep, pltpu.roll(keep, 64, 1))
    del swap
    rows_i = lax.broadcasted_iota(jnp.int32, (ROWS, 128), 0)
    lanes_j = lax.broadcasted_iota(jnp.int32, (ROWS, 128), 1)
    owners_b = jnp.broadcast_to(owners, (ROWS, 128))
    column = jnp.sum(jnp.where(rows_i == lanes_j, owners_b, 0.0), axis=1, keepdims=True)
    earlier = rows_i < jnp.where(lanes_j < 64, lanes_j, lanes_j - 64)
    same = jnp.where((column == owners_b) & earlier, 1.0, 0.0)
    slot = owners * CAP + jnp.sum(same, axis=0, keepdims=True)
    slots = jnp.concatenate([slot, slot], axis=1)
    wanted = lax.broadcasted_iota(jnp.int32, (n_x * CAP, 256), 0).astype(F32)
    used = lax.broadcasted_iota(jnp.int32, (n_x * CAP, 256), 1) < 3 * ROWS
    picker[...] = jnp.where((wanted == slots) & used, 1.0, 0.0).astype(jnp.bfloat16)

    for k, (source, target) in enumerate(((elec_in, elec), (magn_in, magn), (perm_in, perm))):
        load(source, target, 0, 6, 0, 3 + k).wait()
    pack_rows_x(OUTER, outer_at, xsend_o)
    pack_rows_y(OUTER, ysend_o)
    finish(0, 0, xrecv_i)
    unpack_rows_x(0, 8, inner_at, xrecv_i)
    finish(0, 1, yrecv_i)
    for copy in exchange(1, ysend_o, yrecv_o, xsend_o, xrecv_o, TOP, ROWS):
        copy.start()
    unpack_rows_y(INNER, yrecv_i, INNER[:8])

    def keep_planes(s, start, stop):
        def keep_plane(p, carry):
            for c in range(3):
                early[s, c, p] = elec[c, FIRST + p, TOP:TOP + ROWS, LEFT:XCOLS]
            return carry

        lax.fori_loop(start, stop, keep_plane, 0)

    def gradient(k, carry):
        p, t = k // 8, lax.rem(k, 8)
        rows = tile_rows(t)
        ext = pl.ds(pl.multiple_of(TOP + t * 8, 8), 8)
        for h in range(2):
            cols = slice(128 * h, 128 * h + 128)
            far = slice(LEFT + 128 * h, LEFT + 128 * h + 128)
            fields_e = [
                [early[0, c, p, rows, cols], early[1, c, p, rows, cols], elec[c, FIRST + p, ext, far]]
                for c in range(3)
            ]
            keep = mask[p, rows, cols].astype(F32)
            for f in range(FREQ):
                total = jnp.zeros((8, 128), F32)
                for part in range(2):
                    w1, w2, w3 = (trig[f, s, part] for s in range(3))
                    for c in range(3):
                        e1, e2, e3 = fields_e[c]
                        total = total + spec[f, part, c, p, rows, cols] * (
                            w1 * e1 + w2 * e2 + w3 * e3
                        )
                masked[p * FREQ + f, ext, far] = total * keep
        return carry

    def send_edges(part):
        lax.fori_loop(part * 16, part * 16 + 16, gradient, 0)
        for side in range(2):
            for odd in range(2):
                parts = jnp.zeros((8, 128), F32)
                for group in range(4):
                    t = 2 * group + odd
                    ext = slice(TOP + t * 8, TOP + t * 8 + 8)
                    for q in range(8):
                        m, target = part * 8 + q, 32 * group + 3 * q
                        if side == 0:
                            piece = roll(masked[m, ext, 256:384], target + 3, 1)
                        else:
                            piece = roll(masked[m, ext, 128:256], target, 1)
                        parts = jnp.where(lane < target, parts, piece)
                ysend_m[part, side, 8 * odd:8 * odd + 8, :] = parts
            for j in range(4):
                start = TOP + ROWS - 8 if side == 0 else TOP
                m = part * 8 + 2 * j
                first = masked[m, start:start + 8, LEFT:XCOLS]
                second = pltpu.roll(masked[m + 1, start:start + 8, LEFT:XCOLS], 3, 0)
                if side == 0:
                    parts = jnp.where(sub < 3, second, first)
                else:
                    parts = jnp.where(sub < 3, first, second)
                xsend_m[part, side, 8 * j:8 * j + 8, :] = parts
        for copy in exchange(
            2 + part, ysend_m.at[part], yrecv_m.at[part], xsend_m.at[part], xrecv_m.at[part], 8, 16
        ):
            copy.start()

    def put_edges(part):
        finish(2 + part, 0, xrecv_m.at[part])
        for side in range(2):
            start = 0 if side == 0 else TOP + ROWS
            for j in range(4):
                m = part * 8 + 2 * j
                parts = xrecv_m[part, side, 8 * j:8 * j + 8, :]
                parts = parts * (has_down if side == 0 else has_up)
                masked[m, start:start + 8, LEFT:XCOLS] = parts
                masked[m + 1, start:start + 8, LEFT:XCOLS] = pltpu.roll(parts, 5, 0)
        finish(2 + part, 1, yrecv_m.at[part])
        for t in range(10):
            if t == 0:
                there, row, shift = has_down, 0, 96
            elif t == 9:
                there, row, shift = has_up, 24, 0
            else:
                there, row, shift = 1.0, 8 + 8 * ((t - 1) % 2), 32 * ((t - 1) // 2)
            low = yrecv_m[part, 0, row:row + 8, :] * (there * has_left)
            high = yrecv_m[part, 1, row:row + 8, :] * (there * has_right)
            for q in range(8):
                target = shift + 3 * q
                masked[part * 8 + q, 8 * t:8 * t + 8, 0:128] = jnp.where(
                    lane < 64, roll(high, -target, 1), roll(low, 125 - target, 1)
                )

    magnetic(3, 10)
    electric(4, 10)
    keep_planes(0, 0, DP)
    magnetic(4, 9)
    electric(5, 9)
    keep_planes(1, 0, 3)
    magnetic(5, 8)
    electric(6, 8)
    for copy in loads_s:
        copy.wait()
    send_edges(0)
    unpack_rows_x(8, 10, inner_at, xrecv_i)
    unpack_rows_y(INNER, yrecv_i, INNER[8:])
    magnetic(10, 12)
    electric(10, 12)
    magnetic(9, 11)
    electric(9, 11)
    keep_planes(1, 3, DP)
    magnetic(8, 10)
    electric(8, 10)
    send_edges(1)

    def filter_plane(m, carry):
        for t in range(10):
            value = masked[m, 8 * t:8 * t + 8, :]
            center = value[:, LEFT:XCOLS]
            pairs = [
                (pltpu.roll(value, b, 1) + pltpu.roll(value, XCOLS - b, 1))[:, LEFT:XCOLS]
                for b in range(1, RADIUS + 1)
            ]
            for a in range(RADIUS + 1):
                if a == 0 and t in (0, 9):
                    continue
                total = weight(a, 0) * center
                for b in range(1, RADIUS + 1):
                    if weight(a, b) > 0.0:
                        total = total + weight(a, b) * pairs[b - 1]
                fold[a, 8 * t:8 * t + 8, :] = total
        for t in range(1, 9):
            total = fold[0, 8 * t:8 * t + 8, :]
            for a in range(1, RADIUS + 1):
                here = fold[a, 8 * t:8 * t + 8, :]
                after = fold[a, 8 * t + 8:8 * t + 16, :]
                before = fold[a, 8 * t - 8:8 * t, :]
                total = total + pltpu.roll(jnp.where(sub < a, after, here), 8 - a, 0)
                total = total + pltpu.roll(jnp.where(sub >= 8 - a, before, here), a, 0)
            plane_out[8 * t - 8:8 * t, :] = total * inverse_norm[8 * t - 8:8 * t, :]
        value = plane_out[...]
        high = value.astype(jnp.bfloat16)
        rest = value - high.astype(F32)
        middle = rest.astype(jnp.bfloat16)
        low = (rest - middle.astype(F32)).astype(jnp.bfloat16)
        stacked = jnp.concatenate([high, middle, low, jnp.zeros_like(low)], axis=0)
        picked = jnp.dot(picker[...], stacked, preferred_element_type=F32)
        packed[lax.rem(m, FREQ), m // FREQ] = picked
        return carry

    mine = pl.ds(pl.multiple_of(gx * CAP, CAP), CAP)
    for p in range(DP):
        if p % 2 == 0:
            put_edges(p // 2)
        lax.fori_loop(p * FREQ, p * FREQ + FREQ, filter_plane, 0)
        for k in list(range(n_x // 2, n_x)) + list(range(1, n_x // 2)):
            owner = gx ^ k
            theirs = pl.ds(pl.multiple_of(owner * CAP, CAP), CAP)
            pltpu.make_async_remote_copy(
                src_ref=packed.at[:, p, theirs], dst_ref=owned_out.at[:, p, mine],
                send_sem=route_sem.at[0], recv_sem=route_sem.at[1],
                device_id=(owner, gy), device_id_type=MESH,
            ).start()
        pltpu.make_async_copy(
            packed.at[:, p, mine], owned_out.at[:, p, mine], route_sem.at[2]
        ).start()

    finish(1, 0, xrecv_o)
    finish(1, 1, yrecv_o)
    unpack_rows_x(0, len(OUTER), outer_at, xrecv_o)
    unpack_rows_y(OUTER, yrecv_o, OUTER)
    for s in range(3):
        magnetic(12 - s, NZ)
        magnetic(0, 3 + s)
        electric(12 - s, NZ)
        electric(0, 4 + s)
    saves = [
        pltpu.make_async_copy(elec.at[:, pl.ds(0, NZ), own_r, own_c], elec_out, save_sem.at[0]),
        pltpu.make_async_copy(magn.at[:, pl.ds(1, NZ), own_r, own_c], magn_out, save_sem.at[1]),
    ]
    for copy in saves:
        copy.start()
    for copy in saves:
        copy.wait()
    others = pl.ds(0, (n_x - 1) * CAP)
    pltpu.make_async_remote_copy(
        src_ref=packed.at[:, :, others], dst_ref=owned_out.at[:, :, others],
        send_sem=route_sem.at[0], recv_sem=route_sem.at[1],
        device_id=(x_up, gy), device_id_type=MESH,
    ).wait()
    first = pl.ds(0, CAP)
    pltpu.make_async_copy(packed.at[:, :, first], owned_out.at[:, :, first], route_sem.at[2]).wait()


def save(elec, magn, owned, elec_out, magn_out, owned_out, sem):
    copies = [
        pltpu.make_async_copy(elec, elec_out, sem.at[0]),
        pltpu.make_async_copy(magn, magn_out, sem.at[1]),
        pltpu.make_async_copy(owned, owned_out, sem.at[2]),
    ]
    for copy in copies:
        copy.start()
    for copy in copies:
        copy.wait()


def body(n_x, n_y, elec, magn, perm, spec, freq, mask, owner):
    hbm = pl.BlockSpec(memory_space=pltpu.HBM)
    vmem = pl.BlockSpec(memory_space=pltpu.VMEM)
    any_space = pl.BlockSpec(memory_space=pl.ANY)
    buf = pltpu.VMEM
    sem = pltpu.SemaphoreType.DMA
    held = pl.pallas_call(
        functools.partial(kernel, n_x, n_y),
        out_shape=(
            buf((3, NZ, ROWS, COLS), F32),
            buf((3, NZ, ROWS, COLS), F32),
            buf((FREQ, DP, n_x * CAP, COLS), F32),
        ),
        in_specs=[hbm] * 7,
        out_specs=(any_space,) * 3,
        scratch_shapes=[
            buf((3, NZ + 1, XROWS, XCOLS), F32),
            buf((3, NZ + 1, XROWS, XCOLS), F32),
            buf((3, NZ, XROWS, XCOLS), F32),
            buf((FREQ, 2, 3, DP, ROWS, COLS), F32),
            pltpu.SMEM((FREQ,), F32),
            buf((DP, ROWS, COLS), jnp.int32),
            buf((8, 128), jnp.int32),
            buf((FREQ, 3, 2, 8, 128), F32),
            buf((2, 3, DP, ROWS, COLS), F32),
            buf((FREQ * DP, XROWS, XCOLS), F32),
            buf((ROWS, COLS), F32),
            buf((n_x * CAP, 256), jnp.bfloat16),
            buf((RADIUS + 1, XROWS, COLS), F32),
            buf((ROWS, COLS), F32),
            buf((FREQ, DP, n_x * CAP, COLS), F32),
            buf((2, ROWS, 256), F32), buf((2, XROWS, 256), F32),
            buf((2, len(INNER), 24, COLS), F32), buf((2, len(INNER), 24, COLS), F32),
            buf((2, ROWS, 256), F32), buf((2, XROWS, 256), F32),
            buf((2, len(OUTER), 24, COLS), F32), buf((2, len(OUTER), 24, COLS), F32),
            buf((2, 2, 16, 128), F32), buf((2, 2, 32, 128), F32),
            buf((2, 2, 32, COLS), F32), buf((2, 2, 32, COLS), F32),
            sem((10,)), sem((2,)), sem((4, 2)), sem((4, 2)), sem((3,)),
        ],
        compiler_params=pltpu.CompilerParams(
            collective_id=0, has_side_effects=True, vmem_limit_bytes=40 << 20
        ),
        name="adjoint",
    )(*[pltpu.with_memory_space_constraint(v, pltpu.HBM) for v in (elec, magn, perm, spec, freq, mask, owner.reshape(8, 128))])
    return pl.pallas_call(
        save,
        out_shape=(
            jax.ShapeDtypeStruct((3, NZ, ROWS, COLS), F32),
            jax.ShapeDtypeStruct((3, NZ, ROWS, COLS), F32),
            jax.ShapeDtypeStruct((FREQ, DP, n_x * CAP, COLS), F32),
        ),
        in_specs=[vmem] * 3,
        out_specs=(hbm,) * 3,
        scratch_shapes=[sem((3,))],
        compiler_params=pltpu.CompilerParams(vmem_limit_bytes=1 << 20),
        name="save",
    )(*held)


def solution(mesh):
    placed = (
        P(None, None, "gx", "gy"),
        P(None, None, "gx", "gy"),
        P(None, None, "gx", "gy"),
        P(None, None, None, None, "gx", "gy"),
        P(),
        P(None, "gx", "gy"),
        P(),
    )
    return jax.shard_map(
        functools.partial(body, mesh.shape["gx"], mesh.shape["gy"]),
        mesh=mesh,
        in_specs=placed,
        out_specs=(P(None, None, "gx", "gy"), P(None, None, "gx", "gy"), P(None, None, "gx", "gy")),
        check_vma=False,
    )
```
